256 devices in a mesh: branch: 8 (over x, core), col: 32 (over z, y).
Axes of the slice: x: 4, y: 4, z: 8, core: 2. Of those that a mesh axis runs over, the one named last changes fastest.
Arguments:
- child_fronts: float32 [8, 4096, 4096], P('branch', None, 'col'), as said below
- extend_map: int32 [8, 14], P('branch'), may hold values from 0 to 15, as said below
- parent_front: float32 [4096, 4096], P('branch', 'col'), as said below
Outputs:
- child_factor: float32 [8, 512, 4096], P('branch', None, 'col')
- parent_factor: float32 [512, 4096], P(None, 'col')
- parent_update: float32 [4096, 4096], P('branch', 'col')
The draws below stay inside these ranges and needn't reach their ends.
Inputs may be any that keep to these rules, and one draw needn't show every extreme that they name: Each row of extend_map names 14 different parent blocks; some row names block 0 and some row names block 15. `child_fronts`: each child front is symmetric and positive definite. `parent_front`: the parent front is symmetric and positive definite.
All inputs are finite; a program needn't handle non-finite values.
Results may differ from the reference program's by a relative error of at most 0.0003.
Values sent between devices are 32-bit elements; how exact they have to be, the bound alone decides.
A program may use at most 128 MiB of HBM per device.

```python
import jax
import jax.numpy as jnp
from jax import lax

BS = 256
NC = 4096
P_SIZE = 512
NP = 4096
PP = 512
UB = 14
NPB = 16
CHILDREN = 8


def gram_front(key, count, order, inner, gain):
    key_factor, key_diag = jax.random.split(key, 2)
    factors = jax.random.randint(key_factor, (count, order, inner), -2, 3).astype(jnp.float32)

    def one_gram(factor):
        return jnp.dot(factor, factor.T, precision=lax.Precision.HIGHEST)
    gram = lax.map(one_gram, factors)
    diag = jax.random.uniform(key_diag, (count, order), jnp.float32, 0.1, 0.4)
    eye = (jnp.arange(order)[:, None] == jnp.arange(order)[None, :]).astype(jnp.float32)
    front = gain / (2.0 * inner) * gram + gain * eye[None] * diag[:, :, None]
    return front


def draw_child_fronts(key, part):
    return gram_front(jax.random.fold_in(key, 11), CHILDREN, NC, NC // 2, 1.0)


def draw_parent_front(key, part):
    return gram_front(jax.random.fold_in(key, 23), 1, NP, NP // 4, 4.0)[0]


def draw_extend_map(key, part):
    keys = jax.random.split(jax.random.fold_in(key, 37), CHILDREN)
    targets = jnp.where(jnp.arange(CHILDREN) % 2 == 0, NPB - 1, 0).astype(jnp.int32)

    def one_row(row_key, target):
        order = jax.random.permutation(row_key, NPB).astype(jnp.int32)
        where_target = jnp.argmax(order == target).astype(jnp.int32)
        return jnp.roll(order, -where_target)[:UB]
    return jax.vmap(one_row)(keys, targets)


def setup_inputs(seed: int = 0) -> dict:
    seeds = jax.random.split(jax.random.key(seed), 4)
    child_fronts = draw_child_fronts(jax.random.fold_in(seeds[3], 71), 0)
    extend_map = draw_extend_map(jax.random.fold_in(seeds[3], 71), 0)
    parent_front = draw_parent_front(jax.random.fold_in(seeds[3], 71), 0)
    return {"child_fronts": child_fronts, "extend_map": extend_map, "parent_front": parent_front}


def outer_rows(left, right):
    return lax.dot_general(left, right, (((0,), (0,)), ((), ())), precision=lax.Precision.HIGHEST)

def solve_lower(lower_factor, rhs):
    return lax.linalg.triangular_solve(lower_factor, rhs, left_side=True, lower=True)

def source_table(blocks):
    hit = blocks[:, None] == jnp.arange(NPB, dtype=jnp.int32)[None, :]
    present = jnp.any(hit, axis=0)
    child_block = jnp.sum(jnp.where(hit, jnp.arange(UB, dtype=jnp.int32)[:, None], 0), axis=0).astype(jnp.int32)
    positions = jnp.arange(NP, dtype=jnp.int32)
    source = (child_block[positions // BS] * BS + positions % BS).astype(jnp.int32)
    keep = present[positions // BS].astype(jnp.float32)
    return (source, keep)

def reference(child_fronts, extend_map, parent_front):

    def one_child(total, inputs):
        front, blocks = inputs
        top = front[:P_SIZE]
        lower_factor = jnp.linalg.cholesky(top[:, :P_SIZE])
        factor = solve_lower(lower_factor, top)
        tail = factor[:, P_SIZE:]
        update = front[P_SIZE:, P_SIZE:] - outer_rows(tail, tail)
        source, keep = source_table(blocks)
        spread = jnp.take(jnp.take(update, source, axis=0), source, axis=1)
        spread = spread * keep[:, None] * keep[None, :]
        return (total + spread, factor)
    summed, factors = lax.scan(one_child, jnp.zeros((NP, NP), jnp.float32), (child_fronts, extend_map))
    assembled = parent_front + summed
    ptop = assembled[:PP]
    plower = jnp.linalg.cholesky(ptop[:, :PP])
    pfactor = solve_lower(plower, ptop)
    pupdate = assembled - outer_rows(pfactor, pfactor)
    return (factors, pfactor, pupdate)
```

```python
import jax
import jax.numpy as jnp
from jax import lax
from jax.experimental import pallas as pl
from jax.experimental.pallas import tpu as pltpu
from jax.sharding import PartitionSpec as P

BS = 256
P_SIZE = 512
NP = 4096
PP = 512
HB = 128
NZ, NY = 8, 4
NH = NZ * NY
LO = 32
F32 = jnp.float32
HI = lax.Precision.HIGHEST
VMEM = pl.BlockSpec(memory_space=pltpu.VMEM)
SMEM = pl.BlockSpec(memory_space=pltpu.SMEM)
ANY = pl.BlockSpec(memory_space=pl.ANY)


def dot(a, b, dims):
    return lax.dot_general(a, b, (dims, ((), ())), precision=HI, preferred_element_type=F32)


def lane(x, i):
    return jnp.broadcast_to(x[:, i : i + 1], (8, 128))


def sub(x, i):
    return jnp.broadcast_to(x[i : i + 1, :], (8, x.shape[1]))


def chol_inv_128(tiles):
    row = lax.broadcasted_iota(jnp.int32, (8, 128), 0)
    col = lax.broadcasted_iota(jnp.int32, (8, 128), 1)
    D = list(tiles)
    E = [jnp.where(col == row + 8 * q, 1.0, 0.0).astype(F32) for q in range(16)]
    for p in range(16):
        a, e = D[p], E[p]
        C = [lane(a, 8 * p + k) for k in range(8)]
        for k in range(8):
            rs = lax.rsqrt(sub(C[k], k))
            l = C[k] * rs
            lm = jnp.where(row > k, l, 0.0)
            for j in range(k + 1, 8):
                C[j] = C[j] - l * sub(l, j)
            ra = sub(a, k) * rs
            re = sub(e, k) * rs
            a = jnp.where(row == k, ra, a - lm * ra)
            e = jnp.where(row == k, re, e - lm * re)
        E[p] = e
        if p < 15:
            at = a.T
            for q in range(p + 1, 16):
                t, u = D[q], E[q]
                for k in range(8):
                    m = jnp.broadcast_to(at[8 * q : 8 * q + 8, k : k + 1], (8, 128))
                    t = t - m * sub(a, k)
                    u = u - m * sub(e, k)
                D[q], E[q] = t, u
    return E


def chol_inverse(s_ref, m_ref):
    r_ = lax.broadcasted_iota(jnp.int32, (512, 512), 0)
    c_ = lax.broadcasted_iota(jnp.int32, (512, 512), 1)
    m_ref[...] = jnp.where(r_ == c_, 1.0, 0.0).astype(F32)
    for b in range(4):
        o = 128 * b
        tiles = [s_ref[o + 8 * q : o + 8 * q + 8, o : o + 128] for q in range(16)]
        W = jnp.concatenate(chol_inv_128(tiles), axis=0)
        if b:
            m_ref[o : o + 128, :o] = dot(W, m_ref[o : o + 128, :o], ((1,), (0,)))
        m_ref[o : o + 128, o : o + 128] = W
        if b < 3:
            R = dot(W, s_ref[o : o + 128, o + 128 :], ((1,), (0,)))
            s_ref[o + 128 :, o + 128 :] -= dot(R, R, ((0,), (0,)))
            m_ref[o + 128 :, : o + 128] -= dot(R, m_ref[o : o + 128, : o + 128], ((0,), (0,)))


def prep_kernel(map_ref, front_ref, send_ref, tt_ref, tab_ref):
    for b in range(NP // BS):
        at = jnp.int32(-1)
        for u in range(14):
            at = jnp.where(map_ref[0, u] == b, u, at)
        keep = (at >= 0).astype(jnp.int32)
        src = jnp.where(at >= 0, 2 * at + 4, 0)
        for half in range(2):
            tab_ref[0, 2 * b + half] = src + half
            tab_ref[1, 2 * b + half] = keep

    @pl.loop(0, NH)
    def _(h):
        s = pl.multiple_of(tab_ref[0, h] * HB, HB)
        keep = tab_ref[1, h].astype(F32)
        send_ref[h] = front_ref[pl.ds(s, HB), :].T * keep

    for k in range(4):
        tt_ref[:, 128 * k : 128 * k + 128] = front_ref[128 * k : 128 * k + 128, :].T


def prep(extend_map, front):
    return pl.pallas_call(
        prep_kernel,
        out_shape=(
            jax.ShapeDtypeStruct((NH, HB, HB), F32),
            jax.ShapeDtypeStruct((HB, P_SIZE), F32),
            jax.ShapeDtypeStruct((2, NH), jnp.int32),
        ),
        in_specs=[SMEM, VMEM],
        out_specs=(VMEM, VMEM, SMEM),
        name="prep",
    )(extend_map, front)


def child_kernel(
    tab_ref, tt_ref, send_ref, g_ref, t_ref,
    all_ref, recv_ref, s_ref, m_ref, p_ref,
    s0y, r0y, s0z, r0z, s1z, r1z, s1y, r1y, s1f, r1f, sf, rf, loc,
):
    me = lax.axis_index("col")
    core = lax.rem(lax.axis_index("branch"), 2)
    z, y = me // NY, lax.rem(me, NY)
    d = 1 - 2 * core

    def at(zz, yy):
        return lax.rem(zz + 2 * NZ, NZ) * NY + lax.rem(yy + NY, NY)

    barrier = pltpu.get_barrier_semaphore()

    @pl.loop(1, NH)
    def _(k):
        pl.semaphore_signal(barrier, inc=1, device_id={"col": lax.rem(me + k, NH)})

    pl.semaphore_wait(barrier, NH - 1)

    def copy(src, dst, ss, rs, to):
        return pltpu.make_async_remote_copy(
            src_ref=src, dst_ref=dst, send_sem=ss, recv_sem=rs, device_id={"col": to}
        )

    lo, hi = pl.ds(0, LO), pl.ds(LO, HB - LO)
    mid = (HB - LO) // 2
    half = (pl.ds(LO, mid), pl.ds(LO + mid, mid))
    own = pltpu.make_async_copy(tt_ref, all_ref.at[me], loc.at[0])
    own.start()
    ownf = pltpu.make_async_copy(send_ref.at[me], recv_ref.at[me], loc.at[1])
    ownf.start()

    order = [0, 1, -1, 2, -2, 3, -3, 4]

    def y1(i, side, src=None):
        blk = at(z - order[i] * d, y)
        src = all_ref.at[blk, hi] if src is None else src
        return copy(src, all_ref.at[blk, hi], s1y.at[i, side], r1y.at[i, side], at(z, y + (1 if side == 0 else -1)))

    def recv_y1(i, side):
        blk = at(z - order[i] * d, y - (1 if side == 0 else -1))
        return copy(all_ref.at[blk, hi], all_ref.at[blk, hi], s1y.at[i, side], r1y.at[i, side], me)

    def y1f(i, side):
        blk = at(z - order[i] * d, y - (1 if side == 0 else -1))
        ref = all_ref.at[blk, half[side]]
        return copy(ref, ref, s1f.at[i, side], r1f.at[i, side], at(z, y + (1 if side == 0 else -1)))

    def recv_y1f(i, side):
        blk = at(z - order[i] * d, y + 2)
        ref = all_ref.at[blk, half[side]]
        return copy(ref, ref, s1f.at[i, side], r1f.at[i, side], me)

    def y0(k, src):
        return copy(src, all_ref.at[me, lo], s0y.at[k - 1], r0y.at[k - 1], at(z, y + k))

    def recv_y0(k):
        ref = all_ref.at[at(z, y - k), lo]
        return copy(ref, ref, s0y.at[k - 1], r0y.at[k - 1], me)

    def z0(i):
        o = order[i]
        zz = lax.rem(z - o * d + 2 * NZ, NZ) * NY
        ref = all_ref.at[pl.ds(zz, NY), lo]
        return ref, zz

    fwd, bwd = [0, 1, 3, 5, 7], [0, 2, 4, 6]

    def z1_send(chain, n, src=None):
        i, slot = chain[n], chain[n + 1]
        step = d if chain is fwd else -d
        blk = at(z - order[i] * d, y)
        src = all_ref.at[blk, hi] if src is None else src
        return copy(src, all_ref.at[blk, hi], s1z.at[slot - 1], r1z.at[slot - 1], at(z + step, y))

    def z1_recv(slot):
        ref = all_ref.at[at(z - order[slot] * d, y), hi]
        return copy(ref, ref, s1z.at[slot - 1], r1z.at[slot - 1], me)

    def z0_send(chain, n):
        i, slot = chain[n], chain[n + 1]
        step = d if chain is fwd else -d
        ref, _ = z0(i)
        return copy(ref, ref, s0z.at[slot - 1], r0z.at[slot - 1], at(z + step, y))

    def z0_recv(slot):
        ref, _ = z0(slot)
        return copy(ref, ref, s0z.at[slot - 1], r0z.at[slot - 1], me)

    sends = []

    def go(c):
        c.start()
        sends.append(c)

    go(z1_send(fwd, 0, tt_ref.at[hi]))
    go(z1_send(bwd, 0, tt_ref.at[hi]))
    for k in (1, 3, 2):
        go(y0(k, tt_ref.at[lo]))
    for side in (0, 1):
        go(y1(0, side, tt_ref.at[hi]))
    own.wait()
    for k in (1, 3, 2):
        recv_y0(k).wait_recv()
    go(z0_send(fwd, 0))
    go(z0_send(bwd, 0))
    for n in range(1, 5):
        for chain in (fwd, bwd):
            if n < len(chain):
                slot = chain[n]
                z1_recv(slot).wait_recv()
                if n + 1 < len(chain):
                    go(z1_send(chain, n))
                for side in (0, 1):
                    go(y1(slot, side))
        for i in {1: (0,), 2: (1, 2), 3: (3, 4), 4: (5, 6)}[n]:
            for side in (0, 1):
                recv_y1(i, side).wait_recv()
                go(y1f(i, side))
        for chain in (fwd, bwd):
            if n < len(chain):
                z0_recv(chain[n]).wait_recv()
                if n + 1 < len(chain):
                    go(z0_send(chain, n))
    for side in (0, 1):
        recv_y1(7, side).wait_recv()
        go(y1f(7, side))

    def fsend(k):
        to = lax.rem(me + k, NH)
        return copy(send_ref.at[to], recv_ref.at[me], sf.at[k - 1], rf.at[k - 1], to)

    def frecv(k):
        frm = lax.rem(me + NH - k, NH)
        return copy(send_ref.at[frm], recv_ref.at[frm], sf.at[k - 1], rf.at[k - 1], frm)

    @pl.loop(1, NH)
    def _(k):
        fsend(k).start()

    for i in range(8):
        for side in (0, 1):
            recv_y1f(i, side).wait_recv()

    for j in range(4):
        s_ref[128 * j : 128 * j + 128, :] = all_ref[j]
    chol_inverse(s_ref, m_ref)
    M = m_ref[...]
    g_ref[...] = dot(M, all_ref[me], ((1,), (1,)))
    src = tab_ref[0, me]
    Y = dot(M, all_ref[src], ((1,), (1,)))
    s_ref[:, :HB] = dot(M, Y, ((0,), (0,)))

    @pl.loop(0, NH // 4)
    def _(i):
        rows = all_ref[pl.ds(4 * i, 4)].reshape(4 * HB, P_SIZE)
        p_ref[pl.ds(4 * i, 4)] = dot(rows, s_ref[:, :HB], ((1,), (0,))).reshape(4, HB, HB)

    ownf.wait()

    @pl.loop(1, NH)
    def _(k):
        frecv(k).wait_recv()

    keep_me = tab_ref[1, me].astype(F32)

    @pl.loop(0, NH)
    def _(p):
        q = tab_ref[0, p]
        keep = tab_ref[1, p].astype(F32)
        t_ref[p] = keep * (recv_ref[q] - keep_me * p_ref[q])

    for c in sends:
        c.wait_send()

    @pl.loop(1, NH)
    def _(k):
        fsend(k).wait_send()


def child(tab, tt, send):
    dma = pltpu.SemaphoreType.DMA
    return pl.pallas_call(
        child_kernel,
        out_shape=(
            jax.ShapeDtypeStruct((P_SIZE, HB), F32),
            jax.ShapeDtypeStruct((NH, HB, HB), F32),
        ),
        in_specs=[SMEM, VMEM, VMEM],
        out_specs=(VMEM, VMEM),
        scratch_shapes=[
            pltpu.VMEM((NH, HB, P_SIZE), F32),
            pltpu.VMEM((NH, HB, HB), F32),
            pltpu.VMEM((P_SIZE, P_SIZE), F32),
            pltpu.VMEM((P_SIZE, P_SIZE), F32),
            pltpu.VMEM((NH, HB, HB), F32),
            dma((3,)), dma((3,)), dma((7,)), dma((7,)), dma((7,)), dma((7,)),
            dma((8, 2)), dma((8, 2)), dma((8, 2)), dma((8, 2)),
            dma((31,)), dma((31,)), dma((2,)),
        ],
        compiler_params=pltpu.CompilerParams(
            collective_id=0, has_side_effects=True, vmem_limit_bytes=48 << 20
        ),
        name="child",
    )(tab, tt, send)


def local_chol_kernel(a_ref, m_ref, s_ref):
    s_ref[...] = a_ref[...]
    chol_inverse(s_ref, m_ref)


def local_chol(a):
    return pl.pallas_call(
        local_chol_kernel,
        out_shape=jax.ShapeDtypeStruct((PP, PP), F32),
        in_specs=[VMEM],
        out_specs=VMEM,
        scratch_shapes=[pltpu.VMEM((PP, PP), F32)],
        name="local_chol",
    )(a)


def from_root(x, axis, root):
    mine = lax.axis_index(axis) == root
    return lax.psum(jnp.where(mine, x, jnp.zeros_like(x)), axis)


def on_device(child_fronts, extend_map, parent_front):
    front = child_fronts[0]
    send, tt, tab = prep(extend_map, front)
    child_mine, strip = child(tab, tt, send)
    summed = lax.psum_scatter(strip.reshape(NP, HB), "branch", scatter_dimension=0, tiled=True)
    assembled = parent_front + summed
    nrows, pcols = parent_front.shape
    row_start = lax.axis_index("branch") * nrows
    top_mine = from_root(assembled, "branch", 0)
    ptop = lax.all_gather(top_mine, "col", axis=1, tiled=True)
    M = local_chol(ptop[:, :PP])
    parent_mine = dot(M, top_mine, ((1,), (0,)))
    Z = dot(M, parent_mine, ((0,), (0,)))
    rows = lax.dynamic_slice_in_dim(ptop, row_start, nrows, 1)
    result = assembled - dot(rows, Z, ((0,), (0,)))
    return (child_mine[None], parent_mine, result)


def solution(mesh):
    in_specs = (P("branch", None, "col"), P("branch", None), P("branch", "col"))
    out_specs = (P("branch", None, "col"), P(None, "col"), P("branch", "col"))
    return jax.shard_map(
        on_device, mesh=mesh, in_specs=in_specs, out_specs=out_specs, check_vma=False
    )
```

```python
import jax
import jax.numpy as jnp
from jax import lax
from jax.experimental import pallas as pl
from jax.experimental.pallas import tpu as pltpu
from jax.sharding import PartitionSpec as P

BS = 256
P_SIZE = 512
NP = 4096
PP = 512
HB = 128
NZ, NY = 8, 4
NH = NZ * NY
LO = 32
F32 = jnp.float32
HI = lax.Precision.HIGHEST
VMEM = pl.BlockSpec(memory_space=pltpu.VMEM)
SMEM = pl.BlockSpec(memory_space=pltpu.SMEM)
ANY = pl.BlockSpec(memory_space=pl.ANY)


def dot(a, b, dims):
    return lax.dot_general(a, b, (dims, ((), ())), precision=HI, preferred_element_type=F32)


def lane(x, i):
    return jnp.broadcast_to(x[:, i : i + 1], (8, 128))


def sub(x, i):
    return jnp.broadcast_to(x[i : i + 1, :], (8, x.shape[1]))


def chol_inv_128(tiles, hook=None):
    row = lax.broadcasted_iota(jnp.int32, (8, 128), 0)
    col = lax.broadcasted_iota(jnp.int32, (8, 128), 1)
    D = list(tiles)
    E = [jnp.where(col == row + 8 * q, 1.0, 0.0).astype(F32) for q in range(16)]
    for p in range(16):
        if hook is not None:
            hook(p)
        a, e = D[p], E[p]
        C = [lane(a, 8 * p + k) for k in range(8)]
        for k in range(8):
            rs = lax.rsqrt(sub(C[k], k))
            l = C[k] * rs
            lm = jnp.where(row > k, l, 0.0)
            for j in range(k + 1, 8):
                C[j] = C[j] - l * sub(l, j)
            ra = sub(a, k) * rs
            re = sub(e, k) * rs
            a = jnp.where(row == k, ra, a - lm * ra)
            e = jnp.where(row == k, re, e - lm * re)
        E[p] = e
        if p < 15:
            at = a.T
            for q in range(p + 1, 16):
                t, u = D[q], E[q]
                for k in range(8):
                    m = jnp.broadcast_to(at[8 * q : 8 * q + 8, k : k + 1], (8, 128))
                    t = t - m * sub(a, k)
                    u = u - m * sub(e, k)
                D[q], E[q] = t, u
    return E


def chol_inverse(rows, s_ref, m_ref, hooks=None):
    m_ref[...] = jnp.zeros((512, 512), F32)
    for b in range(4):
        o = 128 * b
        blk = slice(o, o + 128)
        A = rows(b)
        if b:
            A = A - dot(s_ref[:o, blk], s_ref[:o, o:], ((0,), (0,)))
        tiles = [A[8 * q : 8 * q + 8, :128] for q in range(16)]
        s_ref[blk, o:] = A
        W = jnp.concatenate(chol_inv_128(tiles, None if hooks is None else hooks(b)), axis=0)
        m_ref[blk, blk] = W
        if b < 3:
            s_ref[blk, o + 128 :] = dot(W, s_ref[blk, o + 128 :], ((1,), (0,)))
        if b:
            m_ref[blk, :o] = -dot(W, dot(s_ref[:o, blk], m_ref[:o, :o], ((0,), (0,))), ((1,), (0,)))


def prep_kernel(map_ref, front_ref, send_ref, tt_ref, tab_ref):
    for b in range(NP // BS):
        at = jnp.int32(-1)
        for u in range(14):
            at = jnp.where(map_ref[0, u] == b, u, at)
        keep = (at >= 0).astype(jnp.int32)
        src = jnp.where(at >= 0, 2 * at + 4, 0)
        for half in range(2):
            tab_ref[0, 2 * b + half] = src + half
            tab_ref[1, 2 * b + half] = keep

    @pl.loop(0, NH)
    def _(h):
        s = pl.multiple_of(tab_ref[0, h] * HB, HB)
        keep = tab_ref[1, h].astype(F32)
        send_ref[h] = front_ref[pl.ds(s, HB), :].T * keep

    for k in range(4):
        tt_ref[:, 128 * k : 128 * k + 128] = front_ref[128 * k : 128 * k + 128, :].T


def prep(extend_map, front):
    return pl.pallas_call(
        prep_kernel,
        out_shape=(
            jax.ShapeDtypeStruct((NH, HB, HB), F32),
            jax.ShapeDtypeStruct((HB, P_SIZE), F32),
            jax.ShapeDtypeStruct((2, NH), jnp.int32),
        ),
        in_specs=[SMEM, VMEM],
        out_specs=(VMEM, VMEM, SMEM),
        name="prep",
    )(extend_map, front)


def child_kernel(
    tab_ref, tt_ref, send_ref, g_ref, t_ref,
    all_ref, recv_ref, s_ref, m_ref, p_ref,
    s0y, r0y, s0z, r0z, s1z, r1z, s1y, r1y, s1f, r1f, sf, rf, loc,
):
    me = lax.axis_index("col")
    core = lax.rem(lax.axis_index("branch"), 2)
    z, y = me // NY, lax.rem(me, NY)
    d = 1 - 2 * core

    def at(zz, yy):
        return lax.rem(zz + 2 * NZ, NZ) * NY + lax.rem(yy + NY, NY)

    barrier = pltpu.get_barrier_semaphore()

    @pl.loop(1, NH)
    def _(k):
        pl.semaphore_signal(barrier, inc=1, device_id={"col": lax.rem(me + k, NH)})

    pl.semaphore_wait(barrier, NH - 1)

    def copy(src, dst, ss, rs, to):
        return pltpu.make_async_remote_copy(
            src_ref=src, dst_ref=dst, send_sem=ss, recv_sem=rs, device_id={"col": to}
        )

    lo, hi = pl.ds(0, LO), pl.ds(LO, HB - LO)
    mid = (HB - LO) // 2
    half = (pl.ds(LO, mid), pl.ds(LO + mid, mid))
    own = pltpu.make_async_copy(tt_ref, all_ref.at[me], loc.at[0])
    own.start()
    ownf = pltpu.make_async_copy(send_ref.at[me], recv_ref.at[me], loc.at[1])
    ownf.start()

    order = [0, 1, -1, 2, -2, 3, -3, 4]

    def y1(i, side, src=None):
        blk = at(z - order[i] * d, y)
        src = all_ref.at[blk, hi] if src is None else src
        return copy(src, all_ref.at[blk, hi], s1y.at[i, side], r1y.at[i, side], at(z, y + (1 if side == 0 else -1)))

    def recv_y1(i, side):
        blk = at(z - order[i] * d, y - (1 if side == 0 else -1))
        return copy(all_ref.at[blk, hi], all_ref.at[blk, hi], s1y.at[i, side], r1y.at[i, side], me)

    def y1f(i, side):
        blk = at(z - order[i] * d, y - (1 if side == 0 else -1))
        ref = all_ref.at[blk, half[side]]
        return copy(ref, ref, s1f.at[i, side], r1f.at[i, side], at(z, y + (1 if side == 0 else -1)))

    def recv_y1f(i, side):
        blk = at(z - order[i] * d, y + 2)
        ref = all_ref.at[blk, half[side]]
        return copy(ref, ref, s1f.at[i, side], r1f.at[i, side], me)

    def y0(k, src):
        return copy(src, all_ref.at[me, lo], s0y.at[k - 1], r0y.at[k - 1], at(z, y + k))

    def recv_y0(k):
        ref = all_ref.at[at(z, y - k), lo]
        return copy(ref, ref, s0y.at[k - 1], r0y.at[k - 1], me)

    def z0(i):
        o = order[i]
        zz = lax.rem(z - o * d + 2 * NZ, NZ) * NY
        ref = all_ref.at[pl.ds(zz, NY), lo]
        return ref, zz

    fwd, bwd = [0, 1, 3, 5, 7], [0, 2, 4, 6]

    def z1_send(chain, n, src=None):
        i, slot = chain[n], chain[n + 1]
        step = d if chain is fwd else -d
        blk = at(z - order[i] * d, y)
        src = all_ref.at[blk, hi] if src is None else src
        return copy(src, all_ref.at[blk, hi], s1z.at[slot - 1], r1z.at[slot - 1], at(z + step, y))

    def z1_recv(slot):
        ref = all_ref.at[at(z - order[slot] * d, y), hi]
        return copy(ref, ref, s1z.at[slot - 1], r1z.at[slot - 1], me)

    def z0_send(chain, n):
        i, slot = chain[n], chain[n + 1]
        step = d if chain is fwd else -d
        ref, _ = z0(i)
        return copy(ref, ref, s0z.at[slot - 1], r0z.at[slot - 1], at(z + step, y))

    def z0_recv(slot):
        ref, _ = z0(slot)
        return copy(ref, ref, s0z.at[slot - 1], r0z.at[slot - 1], me)

    sends = []

    def go(c):
        c.start()
        sends.append(c)

    go(z1_send(fwd, 0, tt_ref.at[hi]))
    go(z1_send(bwd, 0, tt_ref.at[hi]))
    for k in (1, 3, 2):
        go(y0(k, tt_ref.at[lo]))
    for side in (0, 1):
        go(y1(0, side, tt_ref.at[hi]))
    own.wait()
    for k in (1, 3, 2):
        recv_y0(k).wait_recv()
    go(z0_send(fwd, 0))
    go(z0_send(bwd, 0))
    for n in range(1, 5):
        for chain in (fwd, bwd):
            if n < len(chain):
                slot = chain[n]
                z1_recv(slot).wait_recv()
                if n + 1 < len(chain):
                    go(z1_send(chain, n))
                for side in (0, 1):
                    go(y1(slot, side))
        for i in {1: (0,), 2: (1, 2), 3: (3, 4), 4: (5, 6)}[n]:
            for side in (0, 1):
                recv_y1(i, side).wait_recv()
                go(y1f(i, side))
        for chain in (fwd, bwd):
            if n < len(chain):
                z0_recv(chain[n]).wait_recv()
                if n + 1 < len(chain):
                    go(z0_send(chain, n))
    for side in (0, 1):
        recv_y1(7, side).wait_recv()
        go(y1f(7, side))

    def fsend(k):
        to = lax.rem(me + k, NH)
        return copy(send_ref.at[to], recv_ref.at[me], sf.at[k - 1], rf.at[k - 1], to)

    def frecv(k):
        frm = lax.rem(me + NH - k, NH)
        return copy(send_ref.at[frm], recv_ref.at[frm], sf.at[k - 1], rf.at[k - 1], frm)

    @pl.loop(1, NH)
    def _(k):
        fsend(k).start()

    for i in range(8):
        for side in (0, 1):
            recv_y1f(i, side).wait_recv()

    chol_inverse(lambda b: all_ref[b, :, 128 * b :], s_ref, m_ref)
    M = m_ref[...]
    g_ref[...] = dot(M, all_ref[me], ((1,), (1,)))
    src = tab_ref[0, me]
    Y = dot(M, all_ref[src], ((1,), (1,)))
    s_ref[:, :HB] = dot(M, Y, ((0,), (0,)))

    @pl.loop(0, NH // 4)
    def _(i):
        rows = all_ref[pl.ds(4 * i, 4)].reshape(4 * HB, P_SIZE)
        p_ref[pl.ds(4 * i, 4)] = dot(rows, s_ref[:, :HB], ((1,), (0,))).reshape(4, HB, HB)

    ownf.wait()

    @pl.loop(1, NH)
    def _(k):
        frecv(k).wait_recv()

    keep_me = tab_ref[1, me].astype(F32)

    @pl.loop(0, NH)
    def _(p):
        q = tab_ref[0, p]
        keep = tab_ref[1, p].astype(F32)
        t_ref[p] = keep * (recv_ref[q] - keep_me * p_ref[q])

    for c in sends:
        c.wait_send()

    @pl.loop(1, NH)
    def _(k):
        fsend(k).wait_send()


def child(tab, tt, send):
    dma = pltpu.SemaphoreType.DMA
    return pl.pallas_call(
        child_kernel,
        out_shape=(
            jax.ShapeDtypeStruct((P_SIZE, HB), F32),
            jax.ShapeDtypeStruct((NH, HB, HB), F32),
        ),
        in_specs=[SMEM, VMEM, VMEM],
        out_specs=(VMEM, VMEM),
        scratch_shapes=[
            pltpu.VMEM((NH, HB, P_SIZE), F32),
            pltpu.VMEM((NH, HB, HB), F32),
            pltpu.VMEM((P_SIZE, P_SIZE), F32),
            pltpu.VMEM((P_SIZE, P_SIZE), F32),
            pltpu.VMEM((NH, HB, HB), F32),
            dma((3,)), dma((3,)), dma((7,)), dma((7,)), dma((7,)), dma((7,)),
            dma((8, 2)), dma((8, 2)), dma((8, 2)), dma((8, 2)),
            dma((31,)), dma((31,)), dma((2,)),
        ],
        compiler_params=pltpu.CompilerParams(
            collective_id=0, has_side_effects=True, vmem_limit_bytes=48 << 20
        ),
        name="child",
    )(tab, tt, send)


def parent_kernel(
    t_ref, pf_ref, fac_ref, out_ref,
    rtop, part, top, piv, pan, rx, sx, r2, s_ref, m_ref,
    s_rs, r_rs, s_pf, r_pf, s_ag, r_ag, s_x, r_x, s_2, r_2,
    s_vz, r_vz, s_vy, r_vy, s_nz, r_nz, s_ny, r_ny, loc,
):
    br, me = lax.axis_index("branch"), lax.axis_index("col")
    x, core = br // 2, lax.rem(br, 2)
    z, y = me // NY, lax.rem(me, NY)
    nb = 8

    def along_z(k):
        return lax.rem(z + k, NZ) * NY + y

    def along_y(k):
        return z * NY + lax.rem(y + k, NY)

    barrier = pltpu.get_barrier_semaphore()
    for k in range(1, nb):
        pl.semaphore_signal(barrier, inc=1, device_id={"branch": lax.rem(br + k, nb)})
    for k in range(1, NZ):
        pl.semaphore_signal(barrier, inc=1, device_id={"col": along_z(k)})
    for k in range(1, NY):
        pl.semaphore_signal(barrier, inc=1, device_id={"col": along_y(k)})
    pl.semaphore_wait(barrier, nb - 1 + NZ - 1 + NY - 1)

    def copy(src, dst, ss, rs, **to):
        return pltpu.make_async_remote_copy(
            src_ref=src, dst_ref=dst, send_sem=ss, recv_sem=rs, device_id=to
        )

    def piece(b):
        return pl.ds(pl.multiple_of(16 * b, 16), 16)

    def rs_send(k):
        to = lax.rem(br + k, nb)
        return copy(t_ref.at[pl.ds(0, 4), piece(to)], rtop.at[br], s_rs.at[k - 1], r_rs.at[k - 1], branch=to)

    def rs_recv(k):
        frm = lax.rem(br + nb - k, nb)
        return copy(rtop.at[frm], rtop.at[frm], s_rs.at[k - 1], r_rs.at[k - 1], branch=frm)

    def pf_send(k):
        return copy(pf_ref.at[:, piece(k)], rtop.at[nb], s_pf.at[k - 1], r_pf, branch=jnp.int32(k))

    for k in range(1, nb):
        rs_send(k).start()

    @pl.when(br == 0)
    def _():
        for k in range(1, nb):
            pf_send(k).start()

    def x_send(i):
        grp = 2 * i + 1 - core
        return copy(t_ref.at[pl.ds(4 * grp, 4)], rx.at[i], s_x.at[i], r_x.at[i], branch=br + 1 - 2 * core)

    for i in range(4):
        x_send(i).start()

    own = t_ref[0:4, piece(br), :]
    for k in range(1, nb):
        rs_recv(k).wait_recv()
        own = own + rtop[lax.rem(br + nb - k, nb)]
    part[...] = own

    @pl.when(br == 0)
    def _():
        part[...] += pf_ref[:, 0:16, :]

    @pl.when(br != 0)
    def _():
        copy(rtop.at[nb], rtop.at[nb], s_pf.at[0], r_pf, branch=jnp.int32(0)).wait_recv()
        part[...] += rtop[nb]

    def ag_send(k):
        to = lax.rem(br + k, nb)
        return copy(part, top.at[:, piece(br)], s_ag.at[k - 1], r_ag.at[k - 1], branch=to)

    def ag_recv(k):
        ref = top.at[:, piece(lax.rem(br + nb - k, nb))]
        return copy(part, ref, s_ag.at[k - 1], r_ag.at[k - 1], branch=br)

    for k in range(1, nb):
        ag_send(k).start()
    top[:, piece(br), :] = part[...]
    for k in range(1, nb):
        ag_recv(k).wait_recv()

    def vz(b, k):
        return copy(top.at[b], piv.at[y, b], s_vz.at[b, k - 1], r_vz.at[b], col=along_z(k))

    def vy(b, k):
        return copy(piv.at[y, b], piv.at[y, b], s_vy.at[b, k - 1], r_vy.at[b, k - 1], col=along_y(k))

    def vy_recv(b, k):
        ref = piv.at[lax.rem(y + NY - k, NY), b]
        return copy(ref, ref, s_vy.at[b, k - 1], r_vy.at[b, k - 1], col=me)

    def nz(k):
        return copy(top, pan.at[y], s_nz.at[k - 1], r_nz, col=along_z(k))

    def ny(k):
        return copy(pan.at[y], pan.at[y], s_ny.at[k - 1], r_ny.at[k - 1], col=along_y(k))

    def ny_recv(k):
        ref = pan.at[lax.rem(y + NY - k, NY)]
        return copy(ref, ref, s_ny.at[k - 1], r_ny.at[k - 1], col=me)

    lpiv = pltpu.make_async_copy(top, piv.at[y], loc.at[0])
    lpan = pltpu.make_async_copy(top, pan.at[y], loc.at[1])

    @pl.when(z == 0)
    def _():
        lpiv.start()
        for b in range(4):
            for k in (4, 3, 5, 2, 6, 1, 7):
                vz(b, k).start()
        lpiv.wait()

    @pl.when(z == br)
    def _():
        lpan.start()
        for k in (4, 3, 5, 2, 6, 1, 7):
            nz(k).start()
        lpan.wait()

    def spread(b):
        @pl.when(z != 0)
        def _():
            copy(piv.at[y, b], piv.at[y, b], s_vz.at[b, 0], r_vz.at[b], col=me).wait_recv()

        for k in (2, 1, 3):
            vy(b, k).start()

    def rows(b):
        for k in (1, 3, 2):
            vy_recv(b, k).wait_recv()
        return jnp.concatenate([piv[j, b] for j in range(b, 4)], axis=1)

    def x_recv(i):
        return copy(rx.at[i], rx.at[i], s_x.at[i], r_x.at[i], branch=br)

    def send2(k):
        to = lax.rem(x + k, 4)
        return copy(sx.at[to], r2.at[k - 1], s_2.at[k - 1], r_2.at[k - 1], branch=2 * to + core)

    def hooks(b):
        def hook(p):
            if p == 12 and b < 3:
                spread(b + 1)
            if b == 0 and p == 6:
                for i in range(4):
                    x_recv(i).wait_recv()

                @pl.loop(0, 4)
                def _(i):
                    sx[i] = rx[i] + t_ref[pl.ds(4 * (2 * i + core), 4)]

            if b == 0 and p == 9:
                for k in (2, 1, 3):
                    send2(k).start()
            if b == 3 and p == 4:
                @pl.when(z != br)
                def _():
                    copy(top, pan.at[y], s_nz.at[0], r_nz, col=me).wait_recv()

                for k in (2, 1, 3):
                    ny(k).start()

        return hook

    spread(0)
    chol_inverse(rows, s_ref, m_ref, hooks)
    M = m_ref[...]
    F = dot(M, top[...].reshape(PP, HB), ((1,), (0,)))
    fac_ref[...] = F
    Z = dot(M, F, ((0,), (0,)))
    for k in range(1, 4):
        send2(k).wait_recv()
    for k in (1, 3, 2):
        ny_recv(k).wait_recv()

    s_ref[:, :HB] = Z

    @pl.loop(0, 4)
    def _(j):
        asm = pf_ref[j] + sx[x, j] + r2[0, j] + r2[1, j] + r2[2, j]
        rowsj = pan[j].reshape(PP, HB)
        out_ref[j] = asm - dot(rowsj, s_ref[:, :HB], ((0,), (0,)))

    for k in range(1, nb):
        rs_send(k).wait_send()
        ag_send(k).wait_send()

    @pl.when(br == 0)
    def _():
        for k in range(1, nb):
            pf_send(k).wait_send()

    for i in range(4):
        x_send(i).wait_send()
    for k in range(1, 4):
        send2(k).wait_send()
        ny(k).wait_send()
        for b in range(4):
            vy(b, k).wait_send()

    @pl.when(z == 0)
    def _():
        for b in range(4):
            for k in range(1, NZ):
                vz(b, k).wait_send()

    @pl.when(z == br)
    def _():
        for k in range(1, NZ):
            nz(k).wait_send()


def parent(strip, front):
    dma = pltpu.SemaphoreType.DMA
    return pl.pallas_call(
        parent_kernel,
        out_shape=(
            jax.ShapeDtypeStruct((PP, HB), F32),
            jax.ShapeDtypeStruct((4, HB, HB), F32),
        ),
        in_specs=[VMEM, VMEM],
        out_specs=(VMEM, VMEM),
        scratch_shapes=[
            pltpu.VMEM((9, 4, 16, HB), F32),
            pltpu.VMEM((4, 16, HB), F32),
            pltpu.VMEM((4, HB, HB), F32),
            pltpu.VMEM((4, 4, HB, HB), F32),
            pltpu.VMEM((4, 4, HB, HB), F32),
            pltpu.VMEM((4, 4, HB, HB), F32),
            pltpu.VMEM((4, 4, HB, HB), F32),
            pltpu.VMEM((3, 4, HB, HB), F32),
            pltpu.VMEM((PP, PP), F32),
            pltpu.VMEM((PP, PP), F32),
            dma((7,)), dma((7,)), dma((7,)), dma(()), dma((7,)), dma((7,)),
            dma((4,)), dma((4,)), dma((3,)), dma((3,)),
            dma((4, 7)), dma((4,)), dma((4, 3)), dma((4, 3)),
            dma((7,)), dma(()), dma((3,)), dma((3,)), dma((2,)),
        ],
        compiler_params=pltpu.CompilerParams(
            collective_id=1, has_side_effects=True, vmem_limit_bytes=48 << 20
        ),
        name="parent",
    )(strip, front)


def on_device(child_fronts, extend_map, parent_front):
    front = child_fronts[0]
    send, tt, tab = prep(extend_map, front)
    child_mine, strip = child(tab, tt, send)
    parent_mine, result = parent(strip, parent_front.reshape(4, HB, HB))
    return (child_mine[None], parent_mine, result.reshape(parent_front.shape))


def solution(mesh):
    in_specs = (P("branch", None, "col"), P("branch", None), P("branch", "col"))
    out_specs = (P("branch", None, "col"), P(None, "col"), P("branch", "col"))
    return jax.shard_map(
        on_device, mesh=mesh, in_specs=in_specs, out_specs=out_specs, check_vma=False
    )
```

```python
import jax
import jax.numpy as jnp
from jax import lax
from jax.experimental import pallas as pl
from jax.experimental.pallas import tpu as pltpu
from jax.sharding import PartitionSpec as P

BS = 256
P_SIZE = 512
NP = 4096
PP = 512
HB = 128
NZ, NY = 8, 4
NH = NZ * NY
LO = 32
F32 = jnp.float32
HI = lax.Precision.HIGHEST
VMEM = pl.BlockSpec(memory_space=pltpu.VMEM)
SMEM = pl.BlockSpec(memory_space=pltpu.SMEM)
ANY = pl.BlockSpec(memory_space=pl.ANY)


def dot(a, b, dims):
    return lax.dot_general(a, b, (dims, ((), ())), precision=HI, preferred_element_type=F32)


def lane(x, i):
    return jnp.broadcast_to(x[:, i : i + 1], (8, 128))


def sub(x, i):
    return jnp.broadcast_to(x[i : i + 1, :], (8, x.shape[1]))


def chol_inv_128(tiles, hook=None):
    row = lax.broadcasted_iota(jnp.int32, (8, 128), 0)
    col = lax.broadcasted_iota(jnp.int32, (8, 128), 1)
    D = list(tiles)
    E = [jnp.where(col == row + 8 * q, 1.0, 0.0).astype(F32) for q in range(16)]
    for p in range(16):
        if hook is not None:
            hook(p)
        a, e = D[p], E[p]
        C = [lane(a, 8 * p + k) for k in range(8)]
        for k in range(8):
            rs = lax.rsqrt(sub(C[k], k))
            l = C[k] * rs
            lm = jnp.where(row > k, l, 0.0)
            for j in range(k + 1, 8):
                C[j] = C[j] - l * sub(l, j)
            ra = sub(a, k) * rs
            re = sub(e, k) * rs
            a = jnp.where(row == k, ra, a - lm * ra)
            e = jnp.where(row == k, re, e - lm * re)
        E[p] = e
        if p < 15:
            at = a.T
            for q in range(p + 1, 16):
                t, u = D[q], E[q]
                for k in range(8):
                    m = jnp.broadcast_to(at[8 * q : 8 * q + 8, k : k + 1], (8, 128))
                    t = t - m * sub(a, k)
                    u = u - m * sub(e, k)
                D[q], E[q] = t, u
    return E


def chol_inverse(rows, s_ref, m_ref, hooks=None):
    m_ref[...] = jnp.zeros((512, 512), F32)
    for b in range(4):
        o = 128 * b
        blk = slice(o, o + 128)
        A = rows(b)
        if b:
            A = A - dot(s_ref[:o, blk], s_ref[:o, o:], ((0,), (0,)))
        tiles = [A[8 * q : 8 * q + 8, :128] for q in range(16)]
        s_ref[blk, o:] = A
        W = jnp.concatenate(chol_inv_128(tiles, None if hooks is None else hooks(b)), axis=0)
        m_ref[blk, blk] = W
        if b < 3:
            s_ref[blk, o + 128 :] = dot(W, s_ref[blk, o + 128 :], ((1,), (0,)))
        if b:
            m_ref[blk, :o] = -dot(W, dot(s_ref[:o, blk], m_ref[:o, :o], ((0,), (0,))), ((1,), (0,)))


def chol_inverse_loop(rows, s_ref, m_ref, hook):
    m_ref[...] = jnp.zeros((512, 512), F32)
    s_ref[...] = jnp.zeros((512, 512), F32)

    @pl.loop(0, 4)
    def _(b):
        hook(b)
        o = pl.multiple_of(128 * b, 128)
        blk = pl.ds(o, 128)
        lead = s_ref[:, blk]
        A = rows(b) - dot(lead, s_ref[...], ((0,), (0,)))
        s_ref[blk, :] = A
        tiles = [s_ref[pl.ds(o + 8 * q, 8), blk] for q in range(16)]
        W = jnp.concatenate(chol_inv_128(tiles), axis=0)
        m_ref[blk, :] = -dot(W, dot(lead, m_ref[...], ((0,), (0,))), ((1,), (0,)))
        m_ref[blk, blk] = W
        s_ref[blk, :] = dot(W, A, ((1,), (0,)))


def child_kernel(
    map_ref, front_hbm, g_ref, t_ref,
    front_ref, tt_ref, send_ref, all_ref, recv_ref, s_ref, m_ref, p_ref, tab_ref,
    s0y, r0y, s0z, r0z, s1z, r1z, s1y, r1y, s1f, r1f, sf, rf, loc,
):
    me = lax.axis_index("col")
    core = lax.rem(lax.axis_index("branch"), 2)
    z, y = me // NY, lax.rem(me, NY)
    d = 1 - 2 * core

    top = pltpu.make_async_copy(
        front_hbm.at[pl.ds(0, 4)], front_ref.at[pl.ds(0, 4)], loc.at[0]
    )
    top.start()
    rest = pltpu.make_async_copy(
        front_hbm.at[pl.ds(4, NH - 4)], front_ref.at[pl.ds(4, NH - 4)], loc.at[1]
    )
    rest.start()

    def at(zz, yy):
        return lax.rem(zz + 2 * NZ, NZ) * NY + lax.rem(yy + NY, NY)

    barrier = pltpu.get_barrier_semaphore()

    @pl.loop(1, NH)
    def _(k):
        pl.semaphore_signal(barrier, inc=1, device_id={"col": lax.rem(me + k, NH)})

    for b in range(NP // BS):
        at_u = jnp.int32(-1)
        for u in range(14):
            at_u = jnp.where(map_ref[0, u] == b, u, at_u)
        keep = (at_u >= 0).astype(jnp.int32)
        src = jnp.where(at_u >= 0, 2 * at_u + 4, 0)
        for part in range(2):
            tab_ref[0, 2 * b + part] = src + part
            tab_ref[1, 2 * b + part] = keep

    top.wait()
    for k in range(4):
        tt_ref[:, 128 * k : 128 * k + 128] = front_ref[k].T

    pl.semaphore_wait(barrier, NH - 1)

    def copy(src, dst, ss, rs, to):
        return pltpu.make_async_remote_copy(
            src_ref=src, dst_ref=dst, send_sem=ss, recv_sem=rs, device_id={"col": to}
        )

    lo, hi = pl.ds(0, LO), pl.ds(LO, HB - LO)
    mid = (HB - LO) // 2
    half = (pl.ds(LO, mid), pl.ds(LO + mid, mid))
    own = pltpu.make_async_copy(tt_ref, all_ref.at[me], loc.at[2])
    own.start()

    order = [0, 1, -1, 2, -2, 3, -3, 4]
    fwd, bwd = [0, 1, 3, 5, 7], [0, 2, 4, 6]

    def behind(i):
        if isinstance(i, int):
            return order[i]
        return ((i + 1) // 2) * (2 * lax.rem(i, 2) - 1)

    def z1_send(chain, n, src=None):
        i, slot = chain[n], chain[n + 1]
        step = d if chain is fwd else -d
        blk = at(z - order[i] * d, y)
        src = all_ref.at[blk, hi] if src is None else src
        return copy(src, all_ref.at[blk, hi], s1z.at[slot - 1], r1z.at[slot - 1], at(z + step, y))

    def z1_recv(slot):
        ref = all_ref.at[at(z - order[slot] * d, y), hi]
        return copy(ref, ref, s1z.at[slot - 1], r1z.at[slot - 1], me)

    def y1(i, side, src=None):
        blk = at(z - behind(i) * d, y)
        src = all_ref.at[blk, hi] if src is None else src
        return copy(src, all_ref.at[blk, hi], s1y.at[i, side], r1y.at[i, side], at(z, y + 1 - 2 * side))

    def y1_recv(i, side):
        ref = all_ref.at[at(z - behind(i) * d, y - 1 + 2 * side), hi]
        return copy(ref, ref, s1y.at[i, side], r1y.at[i, side], me)

    def y1f(i, side):
        ref = all_ref.at[at(z - behind(i) * d, y - 1 + 2 * side), half[side]]
        return copy(ref, ref, s1f.at[i, side], r1f.at[i, side], at(z, y + 1 - 2 * side))

    def y1f_recv(i, side):
        ref = all_ref.at[at(z - behind(i) * d, y + 2), half[side]]
        return copy(ref, ref, s1f.at[i, side], r1f.at[i, side], me)

    def y0(k, src):
        return copy(src, all_ref.at[me, lo], s0y.at[k - 1], r0y.at[k - 1], at(z, y + k))

    def y0_recv(k):
        ref = all_ref.at[at(z, y - k), lo]
        return copy(ref, ref, s0y.at[k - 1], r0y.at[k - 1], me)

    def bundle(i):
        return all_ref.at[pl.ds(at(z - order[i] * d, 0), NY), lo]

    def z0_send(chain, n):
        i, slot = chain[n], chain[n + 1]
        step = d if chain is fwd else -d
        return copy(bundle(i), bundle(i), s0z.at[slot - 1], r0z.at[slot - 1], at(z + step, y))

    def z0_recv(slot):
        return copy(bundle(slot), bundle(slot), s0z.at[slot - 1], r0z.at[slot - 1], me)

    def fsend(k):
        to = lax.rem(me + k, NH)
        return copy(send_ref.at[to], recv_ref.at[me], sf.at[k - 1], rf.at[k - 1], to)

    def frecv(k):
        frm = lax.rem(me + NH - k, NH)
        return copy(send_ref.at[frm], recv_ref.at[frm], sf.at[k - 1], rf.at[k - 1], frm)

    def picked(h):
        return front_ref[tab_ref[0, h]].T * tab_ref[1, h].astype(F32)

    def prepare(first, last):
        @pl.loop(first, last)
        def _(k):
            h = lax.rem(me + k, NH)
            send_ref[h] = picked(h)

    def start_f(first, last):
        @pl.loop(first, last)
        def _(k):
            fsend(k).start()

    sends = []

    def go(c):
        c.start()
        sends.append(c)

    go(z1_send(fwd, 0, tt_ref.at[hi]))
    go(z1_send(bwd, 0, tt_ref.at[hi]))
    for k in (1, 3, 2):
        go(y0(k, tt_ref.at[lo]))
    for side in (0, 1):
        go(y1(0, side, tt_ref.at[hi]))
    rest.wait()
    prepare(1, 12)
    own.wait()
    for k in (1, 3, 2):
        y0_recv(k).wait_recv()
    go(z0_send(fwd, 0))
    go(z0_send(bwd, 0))
    for n in range(1, 5):
        for chain in (fwd, bwd):
            if n < len(chain):
                slot = chain[n]
                z1_recv(slot).wait_recv()
                if n + 1 < len(chain):
                    go(z1_send(chain, n))
                for side in (0, 1):
                    go(y1(slot, side))
        if n == 1:
            prepare(12, NH)
            recv_ref[me] = picked(me)
        for chain in (fwd, bwd):
            if n < len(chain):
                z0_recv(chain[n]).wait_recv()
                if n + 1 < len(chain):
                    go(z0_send(chain, n))
        start_f(1 + 4 * (n - 1), 1 + 4 * n)

    dist = lax.rem(z * d + NZ, NZ)
    i0 = jnp.where(dist <= 4, jnp.where(dist == 0, 0, 2 * dist - 1), 2 * (NZ - dist))
    for side in (0, 1):
        y1_recv(i0, side).wait_recv()
        y1f(i0, side).start()
    start_f(17, NH)
    for side in (0, 1):
        y1f_recv(i0, side).wait_recv()

    def forward(b):
        for n in range(2):
            i = 2 * b + n

            @pl.when(i != i0)
            def _():
                for side in (0, 1):
                    y1_recv(i, side).wait_recv()
                    y1f(i, side).start()

    chol_inverse_loop(lambda b: all_ref[b], s_ref, m_ref, forward)
    M = m_ref[...]
    g_ref[...] = dot(M, all_ref[me], ((1,), (1,)))

    @pl.loop(0, 8)
    def _(i):
        @pl.when(i != i0)
        def _():
            for side in (0, 1):
                y1f_recv(i, side).wait_recv()

    Y = dot(M, all_ref[tab_ref[0, me]], ((1,), (1,)))
    s_ref[:, :HB] = dot(M, Y, ((0,), (0,)))

    @pl.loop(0, NH // 4)
    def _(i):
        rows = all_ref[pl.ds(4 * i, 4)].reshape(4 * HB, P_SIZE)
        p_ref[pl.ds(4 * i, 4)] = dot(rows, s_ref[:, :HB], ((1,), (0,))).reshape(4, HB, HB)

    @pl.loop(1, NH)
    def _(k):
        frecv(k).wait_recv()

    keep_me = tab_ref[1, me].astype(F32)

    @pl.loop(0, NH)
    def _(p):
        q = tab_ref[0, p]
        keep = tab_ref[1, p].astype(F32)
        t_ref[p] = keep * (recv_ref[q] - keep_me * p_ref[q])

    for c in sends:
        c.wait_send()

    @pl.loop(0, 8)
    def _(i):
        for side in (0, 1):
            y1f(i, side).wait_send()

    @pl.loop(1, NH)
    def _(k):
        fsend(k).wait_send()


def child(extend_map, front):
    dma = pltpu.SemaphoreType.DMA
    return pl.pallas_call(
        child_kernel,
        out_shape=(
            jax.ShapeDtypeStruct((P_SIZE, HB), F32),
            jax.ShapeDtypeStruct((NH, HB, HB), F32),
        ),
        in_specs=[SMEM, ANY],
        out_specs=(VMEM, VMEM),
        scratch_shapes=[
            pltpu.VMEM((NH, HB, HB), F32),
            pltpu.VMEM((HB, P_SIZE), F32),
            pltpu.VMEM((NH, HB, HB), F32),
            pltpu.VMEM((NH, HB, P_SIZE), F32),
            pltpu.VMEM((NH, HB, HB), F32),
            pltpu.VMEM((P_SIZE, P_SIZE), F32),
            pltpu.VMEM((P_SIZE, P_SIZE), F32),
            pltpu.VMEM((NH, HB, HB), F32),
            pltpu.SMEM((2, NH), jnp.int32),
            dma((3,)), dma((3,)), dma((7,)), dma((7,)), dma((7,)), dma((7,)),
            dma((8, 2)), dma((8, 2)), dma((8, 2)), dma((8, 2)),
            dma((31,)), dma((31,)), dma((3,)),
        ],
        compiler_params=pltpu.CompilerParams(
            collective_id=0, has_side_effects=True, vmem_limit_bytes=48 << 20
        ),
        name="child",
    )(extend_map, front)


PANEL = {(0, 1): 0, (0, 10): 1, (1, 7): 2, (2, 4): 3, (3, 1): 4}


def parent_kernel(
    t_ref, pf_ref, fac_ref, out_ref,
    rtop, part, top, piv, pan, rx, sx, r2, s_ref, m_ref,
    s_rs, r_rs, s_pf, r_pf, s_ag, r_ag, s_x, r_x, s_2, r_2,
    s_vz, r_vz, s_vy, r_vy, s_nz, r_nz, s_ny, r_ny, loc,
):
    br, me = lax.axis_index("branch"), lax.axis_index("col")
    x, core = br // 2, lax.rem(br, 2)
    z, y = me // NY, lax.rem(me, NY)
    nb = 8

    def along_z(k):
        return lax.rem(z + k, NZ) * NY + y

    def along_y(k):
        return z * NY + lax.rem(y + k, NY)

    barrier = pltpu.get_barrier_semaphore()
    for k in range(1, nb):
        pl.semaphore_signal(barrier, inc=1, device_id={"branch": lax.rem(br + k, nb)})
    for k in range(1, NZ):
        pl.semaphore_signal(barrier, inc=1, device_id={"col": along_z(k)})
    for k in range(1, NY):
        pl.semaphore_signal(barrier, inc=1, device_id={"col": along_y(k)})
    pl.semaphore_wait(barrier, nb - 1 + NZ - 1 + NY - 1)

    def copy(src, dst, ss, rs, **to):
        return pltpu.make_async_remote_copy(
            src_ref=src, dst_ref=dst, send_sem=ss, recv_sem=rs, device_id=to
        )

    def piece(b):
        return pl.ds(pl.multiple_of(16 * b, 16), 16)

    def rs_send(k):
        to = lax.rem(br + k, nb)
        return copy(t_ref.at[pl.ds(0, 4), piece(to)], rtop.at[br], s_rs.at[k - 1], r_rs.at[k - 1], branch=to)

    def rs_recv(k):
        frm = lax.rem(br + nb - k, nb)
        return copy(rtop.at[frm], rtop.at[frm], s_rs.at[k - 1], r_rs.at[k - 1], branch=frm)

    def pf_send(k):
        return copy(pf_ref.at[:, piece(k)], rtop.at[nb], s_pf.at[k - 1], r_pf, branch=jnp.int32(k))

    for k in range(1, nb):
        rs_send(k).start()

    @pl.when(br == 0)
    def _():
        for k in range(1, nb):
            pf_send(k).start()

    def x_send(i):
        grp = 2 * i + 1 - core
        return copy(t_ref.at[pl.ds(4 * grp, 4)], rx.at[i], s_x.at[i], r_x.at[i], branch=br + 1 - 2 * core)

    for i in range(4):
        x_send(i).start()

    own = t_ref[0:4, piece(br), :]
    for k in range(1, nb):
        rs_recv(k).wait_recv()
        own = own + rtop[lax.rem(br + nb - k, nb)]
    part[...] = own

    @pl.when(br == 0)
    def _():
        part[...] += pf_ref[:, 0:16, :]

    @pl.when(br != 0)
    def _():
        copy(rtop.at[nb], rtop.at[nb], s_pf.at[0], r_pf, branch=jnp.int32(0)).wait_recv()
        part[...] += rtop[nb]

    def ag_send(k):
        to = lax.rem(br + k, nb)
        return copy(part, top.at[:, piece(br)], s_ag.at[k - 1], r_ag.at[k - 1], branch=to)

    def ag_recv(k):
        ref = top.at[:, piece(lax.rem(br + nb - k, nb))]
        return copy(part, ref, s_ag.at[k - 1], r_ag.at[k - 1], branch=br)

    for k in range(1, nb):
        ag_send(k).start()
    top[:, piece(br), :] = part[...]
    for k in range(1, nb):
        ag_recv(k).wait_recv()

    def chain(dist):
        step = jnp.where(dist <= 4, 1, NZ - 1)
        return step, jnp.logical_and(dist != 0, jnp.logical_and(dist != 4, dist != 5))

    vstep, vmore = chain(z)
    ndist = lax.rem(z + NZ - br, NZ)
    nstep, nmore = chain(ndist)
    nhops = jnp.minimum(ndist, NZ - ndist)

    def vy(b, k):
        return copy(piv.at[y, b], piv.at[y, b], s_vy.at[b, k - 1], r_vy.at[b, k - 1], col=along_y(k))

    def vy_recv(b, k):
        ref = piv.at[lax.rem(y + NY - k, NY), b]
        return copy(ref, ref, s_vy.at[b, k - 1], r_vy.at[b, k - 1], col=me)

    def ny(k):
        return copy(pan.at[y], pan.at[y], s_ny.at[k - 1], r_ny.at[k - 1], col=along_y(k))

    def ny_recv(k):
        ref = pan.at[lax.rem(y + NY - k, NY)]
        return copy(ref, ref, s_ny.at[k - 1], r_ny.at[k - 1], col=me)

    lpiv = pltpu.make_async_copy(top, piv.at[y], loc.at[0])
    lpan = pltpu.make_async_copy(top, pan.at[y], loc.at[1])

    @pl.when(z == 0)
    def _():
        lpiv.start()
        for b in range(4):
            copy(top.at[b], piv.at[y, b], s_vz.at[b, 0], r_vz.at[b], col=along_z(1)).start()
            copy(top.at[b], piv.at[y, b], s_vz.at[b, 1], r_vz.at[b], col=along_z(7)).start()
        lpiv.wait()

    @pl.when(z == br)
    def _():
        lpan.start()
        copy(top, pan.at[y], s_nz.at[0], r_nz, col=along_z(1)).start()
        copy(top, pan.at[y], s_nz.at[1], r_nz, col=along_z(7)).start()
        lpan.wait()

    def spread(b):
        @pl.when(z != 0)
        def _():
            copy(piv.at[y, b], piv.at[y, b], s_vz.at[b, 0], r_vz.at[b], col=me).wait_recv()

        @pl.when(vmore)
        def _():
            copy(piv.at[y, b], piv.at[y, b], s_vz.at[b, 0], r_vz.at[b], col=along_z(vstep)).start()

        for k in (2, 1, 3):
            vy(b, k).start()

    def panel_step(hops):
        @pl.when(nhops == hops)
        def _():
            if hops:
                copy(top, pan.at[y], s_nz.at[0], r_nz, col=me).wait_recv()

            @pl.when(nmore)
            def _():
                copy(pan.at[y], pan.at[y], s_nz.at[0], r_nz, col=along_z(nstep)).start()

            for k in (2, 1, 3):
                ny(k).start()

    def rows(b):
        for k in (1, 3, 2):
            vy_recv(b, k).wait_recv()
        return jnp.concatenate([piv[j, b] for j in range(b, 4)], axis=1)

    def x_recv(i):
        return copy(rx.at[i], rx.at[i], s_x.at[i], r_x.at[i], branch=br)

    def send2(k):
        to = lax.rem(x + k, 4)
        return copy(sx.at[to], r2.at[k - 1], s_2.at[k - 1], r_2.at[k - 1], branch=2 * to + core)

    def hooks(b):
        def hook(p):
            if p == 12 and b < 3:
                spread(b + 1)
            if b == 0 and p == 6:
                for i in range(4):
                    x_recv(i).wait_recv()

                @pl.loop(0, 4)
                def _(i):
                    sx[i] = rx[i] + t_ref[pl.ds(4 * (2 * i + core), 4)]

            if b == 0 and p == 9:
                for k in (2, 1, 3):
                    send2(k).start()
            if (b, p) in PANEL:
                panel_step(PANEL[b, p])

        return hook

    spread(0)
    chol_inverse(rows, s_ref, m_ref, hooks)
    M = m_ref[...]
    F = dot(M, top[...].reshape(PP, HB), ((1,), (0,)))
    fac_ref[...] = F
    Z = dot(M, F, ((0,), (0,)))
    for k in range(1, 4):
        send2(k).wait_recv()
    for k in (1, 3, 2):
        ny_recv(k).wait_recv()

    s_ref[:, :HB] = Z

    @pl.loop(0, 4)
    def _(j):
        asm = pf_ref[j] + sx[x, j] + r2[0, j] + r2[1, j] + r2[2, j]
        rowsj = pan[j].reshape(PP, HB)
        out_ref[j] = asm - dot(rowsj, s_ref[:, :HB], ((0,), (0,)))

    for k in range(1, nb):
        rs_send(k).wait_send()
        ag_send(k).wait_send()

    @pl.when(br == 0)
    def _():
        for k in range(1, nb):
            pf_send(k).wait_send()

    for i in range(4):
        x_send(i).wait_send()
    for k in range(1, 4):
        send2(k).wait_send()
        ny(k).wait_send()
        for b in range(4):
            vy(b, k).wait_send()

    for b in range(4):
        @pl.when(jnp.logical_or(z == 0, vmore))
        def _():
            copy(top.at[b], piv.at[y, b], s_vz.at[b, 0], r_vz.at[b], col=along_z(vstep)).wait_send()

        @pl.when(z == 0)
        def _():
            copy(top.at[b], piv.at[y, b], s_vz.at[b, 1], r_vz.at[b], col=along_z(7)).wait_send()

    @pl.when(jnp.logical_or(ndist == 0, nmore))
    def _():
        copy(top, pan.at[y], s_nz.at[0], r_nz, col=along_z(nstep)).wait_send()

    @pl.when(ndist == 0)
    def _():
        copy(top, pan.at[y], s_nz.at[1], r_nz, col=along_z(7)).wait_send()


def parent(strip, front):
    dma = pltpu.SemaphoreType.DMA
    return pl.pallas_call(
        parent_kernel,
        out_shape=(
            jax.ShapeDtypeStruct((PP, HB), F32),
            jax.ShapeDtypeStruct((4, HB, HB), F32),
        ),
        in_specs=[VMEM, VMEM],
        out_specs=(VMEM, VMEM),
        scratch_shapes=[
            pltpu.VMEM((9, 4, 16, HB), F32),
            pltpu.VMEM((4, 16, HB), F32),
            pltpu.VMEM((4, HB, HB), F32),
            pltpu.VMEM((4, 4, HB, HB), F32),
            pltpu.VMEM((4, 4, HB, HB), F32),
            pltpu.VMEM((4, 4, HB, HB), F32),
            pltpu.VMEM((4, 4, HB, HB), F32),
            pltpu.VMEM((3, 4, HB, HB), F32),
            pltpu.VMEM((PP, PP), F32),
            pltpu.VMEM((PP, PP), F32),
            dma((7,)), dma((7,)), dma((7,)), dma(()), dma((7,)), dma((7,)),
            dma((4,)), dma((4,)), dma((3,)), dma((3,)),
            dma((4, 2)), dma((4,)), dma((4, 3)), dma((4, 3)),
            dma((2,)), dma(()), dma((3,)), dma((3,)), dma((2,)),
        ],
        compiler_params=pltpu.CompilerParams(
            collective_id=1, has_side_effects=True, vmem_limit_bytes=48 << 20
        ),
        name="parent",
    )(strip, front)


def on_device(child_fronts, extend_map, parent_front):
    front = child_fronts[0]
    child_mine, strip = child(extend_map, front.reshape(NH, HB, HB))
    parent_mine, result = parent(strip, parent_front.reshape(4, HB, HB))
    return (child_mine[None], parent_mine, result.reshape(parent_front.shape))


def solution(mesh):
    in_specs = (P("branch", None, "col"), P("branch", None), P("branch", "col"))
    out_specs = (P("branch", None, "col"), P(None, "col"), P("branch", "col"))
    return jax.shard_map(
        on_device, mesh=mesh, in_specs=in_specs, out_specs=out_specs, check_vma=False
    )
```

```python
import jax
import jax.numpy as jnp
from jax import lax
from jax.experimental import pallas as pl
from jax.experimental.pallas import tpu as pltpu
from jax.sharding import PartitionSpec as P

BS = 256
P_SIZE = 512
NP = 4096
PP = 512
HB = 128
NZ, NY = 8, 4
NH = NZ * NY
LO = 32
F32 = jnp.float32
HI = lax.Precision.HIGHEST
VMEM = pl.BlockSpec(memory_space=pltpu.VMEM)
SMEM = pl.BlockSpec(memory_space=pltpu.SMEM)
ANY = pl.BlockSpec(memory_space=pl.ANY)


def dot(a, b, dims):
    return lax.dot_general(a, b, (dims, ((), ())), precision=HI, preferred_element_type=F32)


def lane(x, i):
    return jnp.broadcast_to(x[:, i : i + 1], (8, 128))


def sub(x, i):
    return jnp.broadcast_to(x[i : i + 1, :], (8, x.shape[1]))


def chol_inv_128(tiles, hook=None):
    row = lax.broadcasted_iota(jnp.int32, (8, 128), 0)
    col = lax.broadcasted_iota(jnp.int32, (8, 128), 1)
    D = list(tiles)
    E = [jnp.where(col == row + 8 * q, 1.0, 0.0).astype(F32) for q in range(16)]
    for p in range(16):
        if hook is not None:
            hook(p)
        a, e = D[p], E[p]
        C = [lane(a, 8 * p + k) for k in range(8)]
        for k in range(8):
            rs = lax.rsqrt(sub(C[k], k))
            l = C[k] * rs
            lm = jnp.where(row > k, l, 0.0)
            for j in range(k + 1, 8):
                C[j] = C[j] - l * sub(l, j)
            ra = sub(a, k) * rs
            re = sub(e, k) * rs
            a = jnp.where(row == k, ra, a - lm * ra)
            e = jnp.where(row == k, re, e - lm * re)
        E[p] = e
        if p < 15:
            at = a.T
            for q in range(p + 1, 16):
                t, u = D[q], E[q]
                for k in range(8):
                    m = jnp.broadcast_to(at[8 * q : 8 * q + 8, k : k + 1], (8, 128))
                    t = t - m * sub(a, k)
                    u = u - m * sub(e, k)
                D[q], E[q] = t, u
    return E


def chol_inverse(rows, s_ref, m_ref, hooks=None):
    m_ref[...] = jnp.zeros((512, 512), F32)
    for b in range(4):
        o = 128 * b
        blk = slice(o, o + 128)
        A = rows(b)
        if b:
            A = A - dot(s_ref[:o, blk], s_ref[:o, o:], ((0,), (0,)))
        tiles = [A[8 * q : 8 * q + 8, :128] for q in range(16)]
        s_ref[blk, o:] = A
        W = jnp.concatenate(chol_inv_128(tiles, None if hooks is None else hooks(b)), axis=0)
        m_ref[blk, blk] = W
        if b < 3:
            s_ref[blk, o + 128 :] = dot(W, s_ref[blk, o + 128 :], ((1,), (0,)))
        if b:
            m_ref[blk, :o] = -dot(W, dot(s_ref[:o, blk], m_ref[:o, :o], ((0,), (0,))), ((1,), (0,)))


def chol_inverse_loop(rows, s_ref, m_ref, hook):
    m_ref[...] = jnp.zeros((512, 512), F32)
    s_ref[...] = jnp.zeros((512, 512), F32)

    @pl.loop(0, 4)
    def _(b):
        hook(b)
        o = pl.multiple_of(128 * b, 128)
        blk = pl.ds(o, 128)
        lead = s_ref[:, blk]
        A = rows(b) - dot(lead, s_ref[...], ((0,), (0,)))
        s_ref[blk, :] = A
        tiles = [s_ref[pl.ds(o + 8 * q, 8), blk] for q in range(16)]
        W = jnp.concatenate(chol_inv_128(tiles), axis=0)
        m_ref[blk, :] = -dot(W, dot(lead, m_ref[...], ((0,), (0,))), ((1,), (0,)))
        m_ref[blk, blk] = W
        s_ref[blk, :] = dot(W, A, ((1,), (0,)))


def child_phase(
    map_ref, front_hbm, g_ref, t_ref,
    front_ref, tt_ref, send_ref, all_ref, recv_ref, s_ref, m_ref, p_ref, tab_ref,
    s0y, r0y, s0z, r0z, s1z, r1z, s1y, r1y, s1f, r1f, sf, rf, loc, first_rows_done,
):
    me = lax.axis_index("col")
    br = lax.axis_index("branch")
    z, y = me // NY, lax.rem(me, NY)
    d = -1

    top = pltpu.make_async_copy(
        front_hbm.at[pl.ds(0, 4)], front_ref.at[pl.ds(0, 4)], loc.at[0]
    )
    top.start()
    rest = pltpu.make_async_copy(
        front_hbm.at[pl.ds(4, NH - 4)], front_ref.at[pl.ds(4, NH - 4)], loc.at[1]
    )
    rest.start()

    def at(zz, yy):
        return lax.rem(zz + 2 * NZ, NZ) * NY + lax.rem(yy + NY, NY)

    barrier = pltpu.get_barrier_semaphore()

    @pl.loop(1, NH)
    def _(k):
        pl.semaphore_signal(barrier, inc=1, device_id={"col": lax.rem(me + k, NH)})

    @pl.loop(1, 8)
    def _(k):
        pl.semaphore_signal(barrier, inc=1, device_id={"branch": lax.rem(br + k, 8)})

    for b in range(NP // BS):
        at_u = jnp.int32(-1)
        for u in range(14):
            at_u = jnp.where(map_ref[0, u] == b, u, at_u)
        keep = (at_u >= 0).astype(jnp.int32)
        src = jnp.where(at_u >= 0, 2 * at_u + 4, 0)
        for part in range(2):
            tab_ref[0, 2 * b + part] = src + part
            tab_ref[1, 2 * b + part] = keep

    top.wait()
    for k in range(4):
        tt_ref[:, 128 * k : 128 * k + 128] = front_ref[k].T

    pl.semaphore_wait(barrier, NH - 1 + 7)

    def copy(src, dst, ss, rs, to):
        return pltpu.make_async_remote_copy(
            src_ref=src, dst_ref=dst, send_sem=ss, recv_sem=rs, device_id={"col": to}
        )

    lo, hi = pl.ds(0, LO), pl.ds(LO, HB - LO)
    mid = (HB - LO) // 2
    half = (pl.ds(LO, mid), pl.ds(LO + mid, mid))
    own = pltpu.make_async_copy(tt_ref, all_ref.at[me], loc.at[2])
    own.start()

    order = [0, 1, -1, 2, -2, 3, -3, 4]
    fwd, bwd = [0, 1, 3, 5, 7], [0, 2, 4, 6]

    def behind(i):
        if isinstance(i, int):
            return order[i]
        return ((i + 1) // 2) * (2 * lax.rem(i, 2) - 1)

    def z1_send(chain, n, src=None):
        i, slot = chain[n], chain[n + 1]
        step = d if chain is fwd else -d
        blk = at(z - order[i] * d, y)
        src = all_ref.at[blk, hi] if src is None else src
        return copy(src, all_ref.at[blk, hi], s1z.at[slot - 1], r1z.at[slot - 1], at(z + step, y))

    def z1_recv(slot):
        ref = all_ref.at[at(z - order[slot] * d, y), hi]
        return copy(ref, ref, s1z.at[slot - 1], r1z.at[slot - 1], me)

    def y1(i, side, src=None):
        blk = at(z - behind(i) * d, y)
        src = all_ref.at[blk, hi] if src is None else src
        return copy(src, all_ref.at[blk, hi], s1y.at[i, side], r1y.at[i, side], at(z, y + 1 - 2 * side))

    def y1_recv(i, side):
        ref = all_ref.at[at(z - behind(i) * d, y - 1 + 2 * side), hi]
        return copy(ref, ref, s1y.at[i, side], r1y.at[i, side], me)

    def y1f(i, side):
        ref = all_ref.at[at(z - behind(i) * d, y - 1 + 2 * side), half[side]]
        return copy(ref, ref, s1f.at[i, side], r1f.at[i, side], at(z, y + 1 - 2 * side))

    def y1f_recv(i, side):
        ref = all_ref.at[at(z - behind(i) * d, y + 2), half[side]]
        return copy(ref, ref, s1f.at[i, side], r1f.at[i, side], me)

    def y0(k, src):
        return copy(src, all_ref.at[me, lo], s0y.at[k - 1], r0y.at[k - 1], at(z, y + k))

    def y0_recv(k):
        ref = all_ref.at[at(z, y - k), lo]
        return copy(ref, ref, s0y.at[k - 1], r0y.at[k - 1], me)

    def bundle(i):
        return all_ref.at[pl.ds(at(z - order[i] * d, 0), NY), lo]

    def z0_send(chain, n):
        i, slot = chain[n], chain[n + 1]
        step = d if chain is fwd else -d
        return copy(bundle(i), bundle(i), s0z.at[slot - 1], r0z.at[slot - 1], at(z + step, y))

    def z0_recv(slot):
        return copy(bundle(slot), bundle(slot), s0z.at[slot - 1], r0z.at[slot - 1], me)

    def fsend(k):
        to = lax.rem(me + k, NH)
        return copy(send_ref.at[to], recv_ref.at[me], sf.at[k - 1], rf.at[k - 1], to)

    def frecv(k):
        frm = lax.rem(me + NH - k, NH)
        return copy(send_ref.at[frm], recv_ref.at[frm], sf.at[k - 1], rf.at[k - 1], frm)

    def picked(h):
        return front_ref[tab_ref[0, h]].T * tab_ref[1, h].astype(F32)

    def prepare(first, last):
        @pl.loop(first, last)
        def _(k):
            h = lax.rem(me + k, NH)
            send_ref[h] = picked(h)

    def start_f(first, last):
        @pl.loop(first, last)
        def _(k):
            fsend(k).start()

    sends = []

    def go(c):
        c.start()
        sends.append(c)

    go(z1_send(fwd, 0, tt_ref.at[hi]))
    go(z1_send(bwd, 0, tt_ref.at[hi]))
    for k in (1, 3, 2):
        go(y0(k, tt_ref.at[lo]))
    for side in (0, 1):
        go(y1(0, side, tt_ref.at[hi]))
    rest.wait()
    prepare(1, 12)
    own.wait()
    for k in (1, 3, 2):
        y0_recv(k).wait_recv()
    go(z0_send(fwd, 0))
    go(z0_send(bwd, 0))
    for n in range(1, 5):
        for chain in (fwd, bwd):
            if n < len(chain):
                slot = chain[n]
                z1_recv(slot).wait_recv()
                if n + 1 < len(chain):
                    go(z1_send(chain, n))
                for side in (0, 1):
                    go(y1(slot, side))
        if n == 1:
            prepare(12, NH)
            recv_ref[me] = picked(me)
        for chain in (fwd, bwd):
            if n < len(chain):
                z0_recv(chain[n]).wait_recv()
                if n + 1 < len(chain):
                    go(z0_send(chain, n))
        start_f(1 + 4 * (n - 1), 1 + 4 * n)

    dist = lax.rem(z * d + NZ, NZ)
    i0 = jnp.where(dist <= 4, jnp.where(dist == 0, 0, 2 * dist - 1), 2 * (NZ - dist))
    for side in (0, 1):
        y1_recv(i0, side).wait_recv()
        y1f(i0, side).start()
    start_f(17, NH)
    for side in (0, 1):
        y1f_recv(i0, side).wait_recv()

    def forward(b):
        for n in range(2):
            i = 2 * b + n

            @pl.when(i != i0)
            def _():
                for side in (0, 1):
                    y1_recv(i, side).wait_recv()
                    y1f(i, side).start()

    chol_inverse_loop(lambda b: all_ref[b], s_ref, m_ref, forward)
    M = m_ref[...]
    g_ref[...] = dot(M, all_ref[me], ((1,), (1,)))

    @pl.loop(0, 8)
    def _(i):
        @pl.when(i != i0)
        def _():
            for side in (0, 1):
                y1f_recv(i, side).wait_recv()

    Y = dot(M, all_ref[tab_ref[0, me]], ((1,), (1,)))
    s_ref[:, :HB] = dot(M, Y, ((0,), (0,)))

    @pl.loop(0, NH // 4)
    def _(i):
        rows = all_ref[pl.ds(4 * i, 4)].reshape(4 * HB, P_SIZE)
        p_ref[pl.ds(4 * i, 4)] = dot(rows, s_ref[:, :HB], ((1,), (0,))).reshape(4, HB, HB)

    @pl.loop(1, NH)
    def _(k):
        frecv(k).wait_recv()

    keep_me = tab_ref[1, me].astype(F32)

    def strip(first, last):
        @pl.loop(first, last)
        def _(p):
            q = tab_ref[0, p]
            keep = tab_ref[1, p].astype(F32)
            t_ref[p] = keep * (recv_ref[q] - keep_me * p_ref[q])

    strip(0, 4)
    first_rows_done()
    strip(4, NH)

    def finish():
        for c in sends:
            c.wait_send()

        @pl.loop(0, 8)
        def _(i):
            for side in (0, 1):
                y1f(i, side).wait_send()

        @pl.loop(1, NH)
        def _(k):
            fsend(k).wait_send()

    return finish


PANEL = {(0, 1): 0, (0, 10): 1, (1, 7): 2, (2, 4): 3, (3, 1): 4}


def front_kernel(
    map_ref, front_hbm, pf_ref, g_ref, fac_ref, out_ref,
    front_ref, tt_ref, send_ref, all_ref, recv_ref, s_ref, m_ref, p_ref, t_ref, tab_ref,
    s0y, r0y, s0z, r0z, s1z, r1z, s1y, r1y, s1f, r1f, sf, rf, cloc,
    rtop, part, top, piv, pan, rx, sx, r2,
    s_rs, r_rs, s_pf, r_pf, s_ag, r_ag, s_x, r_x, s_2, r_2,
    s_vz, r_vz, s_vy, r_vy, s_vc, r_vc, s_nz, r_nz, s_ny, r_ny, loc,
):
    br, me = lax.axis_index("branch"), lax.axis_index("col")
    x, core = br // 2, lax.rem(br, 2)
    z, y = me // NY, lax.rem(me, NY)
    nb = 8

    def along_z(k):
        return lax.rem(z + k, NZ) * NY + y

    def along_y(k):
        return z * NY + lax.rem(y + k, NY)

    def copy(src, dst, ss, rs, **to):
        return pltpu.make_async_remote_copy(
            src_ref=src, dst_ref=dst, send_sem=ss, recv_sem=rs, device_id=to
        )

    def piece(b):
        return pl.ds(pl.multiple_of(16 * b, 16), 16)

    def rs_send(k):
        to = lax.rem(br + k, nb)
        return copy(t_ref.at[pl.ds(0, 4), piece(to)], rtop.at[br], s_rs.at[k - 1], r_rs.at[k - 1], branch=to)

    def rs_recv(k):
        frm = lax.rem(br + nb - k, nb)
        return copy(rtop.at[frm], rtop.at[frm], s_rs.at[k - 1], r_rs.at[k - 1], branch=frm)

    def pf_send(k):
        return copy(pf_ref.at[:, piece(k)], rtop.at[nb], s_pf.at[k - 1], r_pf, branch=jnp.int32(k))

    def start_rows():
        for k in range(1, nb):
            rs_send(k).start()

    finish_child = child_phase(
        map_ref, front_hbm, g_ref, t_ref,
        front_ref, tt_ref, send_ref, all_ref, recv_ref, s_ref, m_ref, p_ref, tab_ref,
        s0y, r0y, s0z, r0z, s1z, r1z, s1y, r1y, s1f, r1f, sf, rf, cloc, start_rows,
    )

    @pl.when(br == 0)
    def _():
        for k in range(1, nb):
            pf_send(k).start()

    def x_send(i):
        grp = 2 * i + 1 - core
        return copy(t_ref.at[pl.ds(4 * grp, 4)], rx.at[i], s_x.at[i], r_x.at[i], branch=br + 1 - 2 * core)

    for i in range(4):
        x_send(i).start()

    own = t_ref[0:4, piece(br), :]
    for k in range(1, nb):
        rs_recv(k).wait_recv()
        own = own + rtop[lax.rem(br + nb - k, nb)]
    part[...] = own

    @pl.when(br == 0)
    def _():
        part[...] += pf_ref[:, 0:16, :]

    @pl.when(br != 0)
    def _():
        copy(rtop.at[nb], rtop.at[nb], s_pf.at[0], r_pf, branch=jnp.int32(0)).wait_recv()
        part[...] += rtop[nb]

    def ag_send(k):
        to = lax.rem(br + k, nb)
        return copy(part, top.at[:, piece(br)], s_ag.at[k - 1], r_ag.at[k - 1], branch=to)

    def ag_recv(k):
        ref = top.at[:, piece(lax.rem(br + nb - k, nb))]
        return copy(part, ref, s_ag.at[k - 1], r_ag.at[k - 1], branch=br)

    for k in range(1, nb):
        ag_send(k).start()
    top[:, piece(br), :] = part[...]
    for k in range(1, nb):
        ag_recv(k).wait_recv()

    def chain(dist):
        step = jnp.where(dist <= 4, 1, NZ - 1)
        return step, jnp.logical_and(dist != 0, jnp.logical_and(dist != 4, dist != 5))

    ndist = lax.rem(z + NZ - br, NZ)
    nstep, nmore = chain(ndist)
    nhops = jnp.minimum(ndist, NZ - ndist)
    hrows = pl.ds(pl.multiple_of(64 * core, 64), 64)
    orows = pl.ds(pl.multiple_of(64 - 64 * core, 64), 64)
    other = br + 1 - 2 * core

    def vz(b, k):
        return copy(top.at[b, hrows], piv.at[y, b, hrows], s_vz.at[b, k - 1], r_vz.at[b], col=along_z(k))

    def vy(b, k):
        ref = piv.at[y, b, hrows]
        return copy(ref, ref, s_vy.at[b, k - 1], r_vy.at[b, k - 1], col=along_y(k))

    def vy_recv(b, k):
        ref = piv.at[lax.rem(y + NY - k, NY), b, hrows]
        return copy(ref, ref, s_vy.at[b, k - 1], r_vy.at[b, k - 1], col=me)

    def vc(b):
        ref = piv.at[:, b, hrows]
        return copy(ref, ref, s_vc.at[b], r_vc.at[b], branch=other)

    def vc_recv(b):
        ref = piv.at[:, b, orows]
        return copy(ref, ref, s_vc.at[b], r_vc.at[b], branch=other)

    def ny(k):
        return copy(pan.at[y], pan.at[y], s_ny.at[k - 1], r_ny.at[k - 1], col=along_y(k))

    def ny_recv(k):
        ref = pan.at[lax.rem(y + NY - k, NY)]
        return copy(ref, ref, s_ny.at[k - 1], r_ny.at[k - 1], col=me)

    lpiv = pltpu.make_async_copy(top.at[:, hrows], piv.at[y, :, hrows], loc.at[0])
    lpan = pltpu.make_async_copy(top, pan.at[y], loc.at[1])

    @pl.when(z == 0)
    def _():
        lpiv.start()
        for b in range(4):
            for k in (4, 5, 3, 6, 2, 7, 1):
                vz(b, k).start()
        lpiv.wait()

    @pl.when(z == br)
    def _():
        lpan.start()
        copy(top, pan.at[y], s_nz.at[0], r_nz, col=along_z(1)).start()
        copy(top, pan.at[y], s_nz.at[1], r_nz, col=along_z(7)).start()
        lpan.wait()

    def spread(b):
        @pl.when(z != 0)
        def _():
            ref = piv.at[y, b, hrows]
            copy(ref, ref, s_vz.at[b, 0], r_vz.at[b], col=me).wait_recv()

        for k in (2, 1, 3):
            vy(b, k).start()

    def panel_step(hops):
        @pl.when(nhops == hops)
        def _():
            if hops:
                copy(top, pan.at[y], s_nz.at[0], r_nz, col=me).wait_recv()

            @pl.when(nmore)
            def _():
                copy(pan.at[y], pan.at[y], s_nz.at[0], r_nz, col=along_z(nstep)).start()

            for k in (2, 1, 3):
                ny(k).start()

    def exchange(b):
        for k in (1, 3, 2):
            vy_recv(b, k).wait_recv()
        vc(b).start()

    def rows(b):
        vc_recv(b).wait_recv()
        return jnp.concatenate([piv[j, b] for j in range(b, 4)], axis=1)

    def x_recv(i):
        return copy(rx.at[i], rx.at[i], s_x.at[i], r_x.at[i], branch=br)

    def send2(k):
        to = lax.rem(x + k, 4)
        return copy(sx.at[to], r2.at[k - 1], s_2.at[k - 1], r_2.at[k - 1], branch=2 * to + core)

    def hooks(b):
        def hook(p):
            if p == 7 and b < 3:
                spread(b + 1)
            if p == 12 and b < 3:
                exchange(b + 1)
            if b == 0 and p == 6:
                for i in range(4):
                    x_recv(i).wait_recv()

                @pl.loop(0, 4)
                def _(i):
                    sx[i] = rx[i] + t_ref[pl.ds(4 * (2 * i + core), 4)]

            if b == 0 and p == 9:
                for k in (2, 1, 3):
                    send2(k).start()
            if (b, p) in PANEL:
                panel_step(PANEL[b, p])

        return hook

    spread(0)
    exchange(0)
    chol_inverse(rows, s_ref, m_ref, hooks)
    M = m_ref[...]
    F = dot(M, top[...].reshape(PP, HB), ((1,), (0,)))
    fac_ref[...] = F
    Z = dot(M, F, ((0,), (0,)))
    for k in range(1, 4):
        send2(k).wait_recv()
    for k in (1, 3, 2):
        ny_recv(k).wait_recv()

    s_ref[:, :HB] = Z

    @pl.loop(0, 4)
    def _(j):
        asm = pf_ref[j] + sx[x, j] + r2[0, j] + r2[1, j] + r2[2, j]
        rowsj = pan[j].reshape(PP, HB)
        out_ref[j] = asm - dot(rowsj, s_ref[:, :HB], ((0,), (0,)))

    for k in range(1, nb):
        rs_send(k).wait_send()
        ag_send(k).wait_send()

    @pl.when(br == 0)
    def _():
        for k in range(1, nb):
            pf_send(k).wait_send()

    for i in range(4):
        x_send(i).wait_send()
    for k in range(1, 4):
        send2(k).wait_send()
        ny(k).wait_send()
        for b in range(4):
            vy(b, k).wait_send()

    @pl.when(z == 0)
    def _():
        for b in range(4):
            for k in range(1, NZ):
                vz(b, k).wait_send()

    for b in range(4):
        vc(b).wait_send()

    @pl.when(jnp.logical_or(ndist == 0, nmore))
    def _():
        copy(top, pan.at[y], s_nz.at[0], r_nz, col=along_z(nstep)).wait_send()

    @pl.when(ndist == 0)
    def _():
        copy(top, pan.at[y], s_nz.at[1], r_nz, col=along_z(7)).wait_send()

    finish_child()


def fronts(extend_map, front, parent_front):
    dma = pltpu.SemaphoreType.DMA
    return pl.pallas_call(
        front_kernel,
        out_shape=(
            jax.ShapeDtypeStruct((P_SIZE, HB), F32),
            jax.ShapeDtypeStruct((PP, HB), F32),
            jax.ShapeDtypeStruct((4, HB, HB), F32),
        ),
        in_specs=[SMEM, ANY, VMEM],
        out_specs=(VMEM, VMEM, VMEM),
        scratch_shapes=[
            pltpu.VMEM((NH, HB, HB), F32),
            pltpu.VMEM((HB, P_SIZE), F32),
            pltpu.VMEM((NH, HB, HB), F32),
            pltpu.VMEM((NH, HB, P_SIZE), F32),
            pltpu.VMEM((NH, HB, HB), F32),
            pltpu.VMEM((P_SIZE, P_SIZE), F32),
            pltpu.VMEM((P_SIZE, P_SIZE), F32),
            pltpu.VMEM((NH, HB, HB), F32),
            pltpu.VMEM((NH, HB, HB), F32),
            pltpu.SMEM((2, NH), jnp.int32),
            dma((3,)), dma((3,)), dma((7,)), dma((7,)), dma((7,)), dma((7,)),
            dma((8, 2)), dma((8, 2)), dma((8, 2)), dma((8, 2)),
            dma((31,)), dma((31,)), dma((3,)),
            pltpu.VMEM((9, 4, 16, HB), F32),
            pltpu.VMEM((4, 16, HB), F32),
            pltpu.VMEM((4, HB, HB), F32),
            pltpu.VMEM((4, 4, HB, HB), F32),
            pltpu.VMEM((4, 4, HB, HB), F32),
            pltpu.VMEM((4, 4, HB, HB), F32),
            pltpu.VMEM((4, 4, HB, HB), F32),
            pltpu.VMEM((3, 4, HB, HB), F32),
            dma((7,)), dma((7,)), dma((7,)), dma(()), dma((7,)), dma((7,)),
            dma((4,)), dma((4,)), dma((3,)), dma((3,)),
            dma((4, 7)), dma((4,)), dma((4, 3)), dma((4, 3)), dma((4,)), dma((4,)),
            dma((2,)), dma(()), dma((3,)), dma((3,)), dma((2,)),
        ],
        compiler_params=pltpu.CompilerParams(
            collective_id=0, has_side_effects=True, vmem_limit_bytes=56 << 20
        ),
        name="fronts",
    )(extend_map, front, parent_front)


def on_device(child_fronts, extend_map, parent_front):
    front = child_fronts[0]
    child_mine, parent_mine, result = fronts(
        extend_map, front.reshape(NH, HB, HB), parent_front.reshape(4, HB, HB)
    )
    return (child_mine[None], parent_mine, result.reshape(parent_front.shape))


def solution(mesh):
    in_specs = (P("branch", None, "col"), P("branch", None), P("branch", "col"))
    out_specs = (P("branch", None, "col"), P(None, "col"), P("branch", "col"))
    return jax.shard_map(
        on_device, mesh=mesh, in_specs=in_specs, out_specs=out_specs, check_vma=False
    )
```

```python
import jax
import jax.numpy as jnp
from jax import lax
from jax.experimental import pallas as pl
from jax.experimental.pallas import tpu as pltpu
from jax.sharding import PartitionSpec as P

BS = 256
P_SIZE = 512
NP = 4096
PP = 512
HB = 128
NZ, NY = 8, 4
NH = NZ * NY
LO = 32
F32 = jnp.float32
HI = lax.Precision.HIGHEST
VMEM = pl.BlockSpec(memory_space=pltpu.VMEM)
SMEM = pl.BlockSpec(memory_space=pltpu.SMEM)
HBM = pl.BlockSpec(memory_space=pltpu.HBM)


def dot(a, b, dims):
    return lax.dot_general(a, b, (dims, ((), ())), precision=HI, preferred_element_type=F32)


def lane(x, i):
    return jnp.broadcast_to(x[:, i : i + 1], (8, 128))


def sub(x, i):
    return jnp.broadcast_to(x[i : i + 1, :], (8, x.shape[1]))


def chol_inv_128(tiles, hook=None):
    row = lax.broadcasted_iota(jnp.int32, (8, 128), 0)
    col = lax.broadcasted_iota(jnp.int32, (8, 128), 1)
    D = list(tiles)
    E = [jnp.where(col == row + 8 * q, 1.0, 0.0).astype(F32) for q in range(16)]
    for p in range(16):
        if hook is not None:
            hook(p)
        a, e = D[p], E[p]
        C = [lane(a, 8 * p + k) for k in range(8)]
        for k in range(8):
            rs = lax.rsqrt(sub(C[k], k))
            l = C[k] * rs
            lm = jnp.where(row > k, l, 0.0)
            for j in range(k + 1, 8):
                C[j] = C[j] - l * sub(l, j)
            ra = sub(a, k) * rs
            re = sub(e, k) * rs
            a = jnp.where(row == k, ra, a - lm * ra)
            e = jnp.where(row == k, re, e - lm * re)
        E[p] = e
        if p < 15:
            at = a.T
            for q in range(p + 1, 16):
                t, u = D[q], E[q]
                for k in range(8):
                    m = jnp.broadcast_to(at[8 * q : 8 * q + 8, k : k + 1], (8, 128))
                    t = t - m * sub(a, k)
                    u = u - m * sub(e, k)
                D[q], E[q] = t, u
    return E


def chol_inverse(rows, s_ref, m_ref, hooks=None):
    m_ref[...] = jnp.zeros((512, 512), F32)
    for b in range(4):
        o = 128 * b
        blk = slice(o, o + 128)
        A = rows(b)
        if b:
            A = A - dot(s_ref[:o, blk], s_ref[:o, o:], ((0,), (0,)))
        tiles = [A[8 * q : 8 * q + 8, :128] for q in range(16)]
        s_ref[blk, o:] = A
        W = jnp.concatenate(chol_inv_128(tiles, None if hooks is None else hooks(b)), axis=0)
        m_ref[blk, blk] = W
        if b < 3:
            s_ref[blk, o + 128 :] = dot(W, s_ref[blk, o + 128 :], ((1,), (0,)))
        if b:
            m_ref[blk, :o] = -dot(W, dot(s_ref[:o, blk], m_ref[:o, :o], ((0,), (0,))), ((1,), (0,)))


def chol_inverse_loop(rows, s_ref, m_ref, hook):
    m_ref[...] = jnp.zeros((512, 512), F32)
    s_ref[...] = jnp.zeros((512, 512), F32)

    @pl.loop(0, 4)
    def _(b):
        hook(b)
        o = pl.multiple_of(128 * b, 128)
        blk = pl.ds(o, 128)
        lead = s_ref[:, blk]
        A = rows(b) - dot(lead, s_ref[...], ((0,), (0,)))
        s_ref[blk, :] = A
        tiles = [s_ref[pl.ds(o + 8 * q, 8), blk] for q in range(16)]
        W = jnp.concatenate(chol_inv_128(tiles), axis=0)
        m_ref[blk, :] = -dot(W, dot(lead, m_ref[...], ((0,), (0,))), ((1,), (0,)))
        m_ref[blk, blk] = W
        s_ref[blk, :] = dot(W, A, ((1,), (0,)))


def child_phase(
    map_ref, front_hbm, g_ref, t_ref,
    front_ref, tt_ref, send_ref, all_ref, recv_ref, s_ref, m_ref, p_ref, tab_ref,
    s0y, r0y, s0z, r0z, s1z, r1z, s1y, r1y, s1f, r1f, sf, rf, loc, first_rows_done,
):
    me = lax.axis_index("col")
    br = lax.axis_index("branch")
    z, y = me // NY, lax.rem(me, NY)
    d = -1

    top = pltpu.make_async_copy(
        front_hbm.at[pl.ds(0, 4)], front_ref.at[pl.ds(0, 4)], loc.at[0]
    )
    top.start()
    rest = pltpu.make_async_copy(
        front_hbm.at[pl.ds(4, NH - 4)], front_ref.at[pl.ds(4, NH - 4)], loc.at[1]
    )
    rest.start()

    def at(zz, yy):
        return lax.rem(zz + 2 * NZ, NZ) * NY + lax.rem(yy + NY, NY)

    barrier = pltpu.get_barrier_semaphore()

    @pl.loop(1, NH)
    def _(k):
        pl.semaphore_signal(barrier, inc=1, device_id={"col": lax.rem(me + k, NH)})

    @pl.loop(1, 8)
    def _(k):
        pl.semaphore_signal(barrier, inc=1, device_id={"branch": lax.rem(br + k, 8)})

    for b in range(NP // BS):
        at_u = jnp.int32(-1)
        for u in range(14):
            at_u = jnp.where(map_ref[0, u] == b, u, at_u)
        keep = (at_u >= 0).astype(jnp.int32)
        src = jnp.where(at_u >= 0, 2 * at_u + 4, 0)
        for part in range(2):
            tab_ref[0, 2 * b + part] = src + part
            tab_ref[1, 2 * b + part] = keep

    top.wait()
    for k in range(4):
        tt_ref[:, 128 * k : 128 * k + 128] = front_ref[k].T

    pl.semaphore_wait(barrier, NH - 1 + 7)

    def copy(src, dst, ss, rs, to):
        return pltpu.make_async_remote_copy(
            src_ref=src, dst_ref=dst, send_sem=ss, recv_sem=rs, device_id={"col": to}
        )

    lo, hi = pl.ds(0, LO), pl.ds(LO, HB - LO)
    mid = (HB - LO) // 2
    half = (pl.ds(LO, mid), pl.ds(LO + mid, mid))
    own = pltpu.make_async_copy(tt_ref, all_ref.at[me], loc.at[2])
    own.start()

    order = [0, 1, -1, 2, -2, 3, -3, 4]
    fwd, bwd = [0, 1, 3, 5, 7], [0, 2, 4, 6]

    def behind(i):
        if isinstance(i, int):
            return order[i]
        return ((i + 1) // 2) * (2 * lax.rem(i, 2) - 1)

    def z1_send(chain, n, src=None):
        i, slot = chain[n], chain[n + 1]
        step = d if chain is fwd else -d
        blk = at(z - order[i] * d, y)
        src = all_ref.at[blk, hi] if src is None else src
        return copy(src, all_ref.at[blk, hi], s1z.at[slot - 1], r1z.at[slot - 1], at(z + step, y))

    def z1_recv(slot):
        ref = all_ref.at[at(z - order[slot] * d, y), hi]
        return copy(ref, ref, s1z.at[slot - 1], r1z.at[slot - 1], me)

    def y1(i, side, src=None):
        blk = at(z - behind(i) * d, y)
        src = all_ref.at[blk, hi] if src is None else src
        return copy(src, all_ref.at[blk, hi], s1y.at[i, side], r1y.at[i, side], at(z, y + 1 - 2 * side))

    def y1_recv(i, side):
        ref = all_ref.at[at(z - behind(i) * d, y - 1 + 2 * side), hi]
        return copy(ref, ref, s1y.at[i, side], r1y.at[i, side], me)

    def y1f(i, side):
        ref = all_ref.at[at(z - behind(i) * d, y - 1 + 2 * side), half[side]]
        return copy(ref, ref, s1f.at[i, side], r1f.at[i, side], at(z, y + 1 - 2 * side))

    def y1f_recv(i, side):
        ref = all_ref.at[at(z - behind(i) * d, y + 2), half[side]]
        return copy(ref, ref, s1f.at[i, side], r1f.at[i, side], me)

    def y0(k, src):
        return copy(src, all_ref.at[me, lo], s0y.at[k - 1], r0y.at[k - 1], at(z, y + k))

    def y0_recv(k):
        ref = all_ref.at[at(z, y - k), lo]
        return copy(ref, ref, s0y.at[k - 1], r0y.at[k - 1], me)

    def bundle(i):
        return all_ref.at[pl.ds(at(z - order[i] * d, 0), NY), lo]

    def z0_send(chain, n):
        i, slot = chain[n], chain[n + 1]
        step = d if chain is fwd else -d
        return copy(bundle(i), bundle(i), s0z.at[slot - 1], r0z.at[slot - 1], at(z + step, y))

    def z0_recv(slot):
        return copy(bundle(slot), bundle(slot), s0z.at[slot - 1], r0z.at[slot - 1], me)

    def fsend(k):
        to = lax.rem(me + k, NH)
        return copy(send_ref.at[to], recv_ref.at[me], sf.at[k - 1], rf.at[k - 1], to)

    def frecv(k):
        frm = lax.rem(me + NH - k, NH)
        return copy(send_ref.at[frm], recv_ref.at[frm], sf.at[k - 1], rf.at[k - 1], frm)

    def picked(h):
        return front_ref[tab_ref[0, h]].T * tab_ref[1, h].astype(F32)

    def prepare(first, last):
        @pl.loop(first, last)
        def _(k):
            h = lax.rem(me + k, NH)
            send_ref[h] = picked(h)

    def start_f(first, last):
        @pl.when(z != 0)
        def _():
            @pl.loop(first, last)
            def _(k):
                fsend(k).start()

    sends = []

    def go(c):
        c.start()
        sends.append(c)

    go(z1_send(fwd, 0, tt_ref.at[hi]))
    go(z1_send(bwd, 0, tt_ref.at[hi]))
    for k in (1, 3, 2):
        go(y0(k, tt_ref.at[lo]))
    for side in (0, 1):
        go(y1(0, side, tt_ref.at[hi]))
    rest.wait()
    prepare(1, 12)
    own.wait()
    for k in (1, 3, 2):
        y0_recv(k).wait_recv()
    go(z0_send(fwd, 0))
    go(z0_send(bwd, 0))
    for n in range(1, 5):
        for chain in (fwd, bwd):
            if n < len(chain):
                slot = chain[n]
                z1_recv(slot).wait_recv()
                if n + 1 < len(chain):
                    go(z1_send(chain, n))
                for side in (0, 1):
                    go(y1(slot, side))
        if n == 1:
            prepare(12, NH)
            recv_ref[me] = picked(me)
        for chain in (fwd, bwd):
            if n < len(chain):
                z0_recv(chain[n]).wait_recv()
                if n + 1 < len(chain):
                    go(z0_send(chain, n))
        start_f(1 + 4 * (n - 1), 1 + 4 * n)

    dist = lax.rem(z * d + NZ, NZ)
    i0 = jnp.where(dist <= 4, jnp.where(dist == 0, 0, 2 * dist - 1), 2 * (NZ - dist))
    for side in (0, 1):
        y1_recv(i0, side).wait_recv()
        y1f(i0, side).start()
    start_f(17, NH)
    for side in (0, 1):
        y1f_recv(i0, side).wait_recv()

    def forward(b):
        for n in range(2):
            i = 2 * b + n

            @pl.when(i != i0)
            def _():
                for side in (0, 1):
                    y1_recv(i, side).wait_recv()
                    y1f(i, side).start()

    chol_inverse_loop(lambda b: all_ref[b], s_ref, m_ref, forward)
    M = m_ref[...]
    g_ref[...] = dot(M, all_ref[me], ((1,), (1,)))

    @pl.loop(0, 8)
    def _(i):
        @pl.when(i != i0)
        def _():
            for side in (0, 1):
                y1f_recv(i, side).wait_recv()

    Y = dot(M, all_ref[tab_ref[0, me]], ((1,), (1,)))
    s_ref[:, :HB] = dot(M, Y, ((0,), (0,)))

    @pl.loop(0, NH // 4)
    def _(i):
        rows = all_ref[pl.ds(4 * i, 4)].reshape(4 * HB, P_SIZE)
        p_ref[pl.ds(4 * i, 4)] = dot(rows, s_ref[:, :HB], ((1,), (0,))).reshape(4, HB, HB)

    @pl.loop(1, NH)
    def _(k):
        @pl.when(lax.rem(me + NH - k, NH) >= NY)
        def _():
            frecv(k).wait_recv()

    keep_me = tab_ref[1, me].astype(F32)

    def strip(first, last):
        @pl.loop(first, last)
        def _(p):
            q = tab_ref[0, p]
            keep = tab_ref[1, p].astype(F32)
            t_ref[p] = keep * (recv_ref[q] - keep_me * p_ref[q])

    strip(0, 4)
    first_rows_done()
    strip(4, NH)

    def finish():
        for c in sends:
            c.wait_send()

        @pl.loop(0, 8)
        def _(i):
            for side in (0, 1):
                y1f(i, side).wait_send()

        @pl.when(z != 0)
        def _():
            @pl.loop(1, NH)
            def _(k):
                fsend(k).wait_send()

    return finish


SLOTS = {(0, 2): 0, (0, 9): 1, (1, 0): 2, (1, 7): 3, (1, 14): 4, (2, 5): 5, (2, 12): 6, (3, 3): 7}


def front_kernel(
    map_ref, front_hbm, pf_ref, g_ref, fac_ref, out_ref,
    front_ref, tt_ref, send_ref, all_ref, recv_ref, s_ref, m_ref, p_ref, t_ref, tab_ref,
    s0y, r0y, s0z, r0z, s1z, r1z, s1y, r1y, s1f, r1f, sf, rf, cloc,
    rtop, part, top, piv, pan, rx, sx, r2,
    s_rs, r_rs, s_pf, r_pf, s_ag, r_ag, s_x, r_x, s_2, r_2,
    s_vz, r_vz, s_vy, r_vy, s_vc, r_vc, s_nz, r_nz, s_ny, r_ny, loc,
):
    br, me = lax.axis_index("branch"), lax.axis_index("col")
    x, core = br // 2, lax.rem(br, 2)
    z, y = me // NY, lax.rem(me, NY)
    nb = 8

    def along_z(k):
        return lax.rem(z + k, NZ) * NY + y

    def along_y(k):
        return z * NY + lax.rem(y + k, NY)

    def copy(src, dst, ss, rs, **to):
        return pltpu.make_async_remote_copy(
            src_ref=src, dst_ref=dst, send_sem=ss, recv_sem=rs, device_id=to
        )

    def piece(b):
        return pl.ds(pl.multiple_of(16 * b, 16), 16)

    def rs_send(k):
        to = lax.rem(br + k, nb)
        return copy(t_ref.at[pl.ds(0, 4), piece(to)], rtop.at[br], s_rs.at[k - 1], r_rs.at[k - 1], branch=to)

    def rs_recv(k):
        frm = lax.rem(br + nb - k, nb)
        return copy(rtop.at[frm], rtop.at[frm], s_rs.at[k - 1], r_rs.at[k - 1], branch=frm)

    def pf_send(k):
        return copy(pf_ref.at[:, piece(k)], rtop.at[nb], s_pf.at[k - 1], r_pf, branch=jnp.int32(k))

    def start_rows():
        for k in range(1, nb):
            rs_send(k).start()

    finish_child = child_phase(
        map_ref, front_hbm, g_ref, t_ref,
        front_ref, tt_ref, send_ref, all_ref, recv_ref, s_ref, m_ref, p_ref, tab_ref,
        s0y, r0y, s0z, r0z, s1z, r1z, s1y, r1y, s1f, r1f, sf, rf, cloc, start_rows,
    )

    @pl.when(br == 0)
    def _():
        for k in range(1, nb):
            pf_send(k).start()

    def x_send(i):
        grp = 2 * i + 1 - core
        return copy(t_ref.at[pl.ds(4 * grp, 4)], rx.at[i], s_x.at[i], r_x.at[i], branch=br + 1 - 2 * core)

    for i in range(4):
        x_send(i).start()

    own = t_ref[0:4, piece(br), :]
    for k in range(1, nb):
        rs_recv(k).wait_recv()
        own = own + rtop[lax.rem(br + nb - k, nb)]
    part[...] = own

    @pl.when(br == 0)
    def _():
        part[...] += pf_ref[:, 0:16, :]

    @pl.when(br != 0)
    def _():
        copy(rtop.at[nb], rtop.at[nb], s_pf.at[0], r_pf, branch=jnp.int32(0)).wait_recv()
        part[...] += rtop[nb]

    def ag_send(k):
        to = lax.rem(br + k, nb)
        return copy(part, top.at[:, piece(br)], s_ag.at[k - 1], r_ag.at[k - 1], branch=to)

    def ag_recv(k):
        ref = top.at[:, piece(lax.rem(br + nb - k, nb))]
        return copy(part, ref, s_ag.at[k - 1], r_ag.at[k - 1], branch=br)

    for k in range(1, nb):
        ag_send(k).start()
    top[:, piece(br), :] = part[...]
    for k in range(1, nb):
        ag_recv(k).wait_recv()

    def chain(dist):
        step = jnp.where(dist <= 4, 1, NZ - 1)
        return step, jnp.logical_and(dist != 0, jnp.logical_and(dist != 4, dist != 5))

    ndist = lax.rem(z + NZ - br, NZ)
    nstep, nmore = chain(ndist)
    nhops = jnp.minimum(ndist, NZ - ndist)
    hrows = pl.ds(pl.multiple_of(64 * core, 64), 64)
    orows = pl.ds(pl.multiple_of(64 - 64 * core, 64), 64)
    other = br + 1 - 2 * core

    def vz(b, k):
        return copy(top.at[b, hrows], piv.at[y, b, hrows], s_vz.at[b, k - 1], r_vz.at[b], col=along_z(k))

    def vy(b, k):
        ref = piv.at[y, b, hrows]
        return copy(ref, ref, s_vy.at[b, k - 1], r_vy.at[b, k - 1], col=along_y(k))

    def vy_recv(b, k):
        ref = piv.at[lax.rem(y + NY - k, NY), b, hrows]
        return copy(ref, ref, s_vy.at[b, k - 1], r_vy.at[b, k - 1], col=me)

    def vc(b):
        ref = piv.at[:, b, hrows]
        return copy(ref, ref, s_vc.at[b], r_vc.at[b], branch=other)

    def vc_recv(b):
        ref = piv.at[:, b, orows]
        return copy(ref, ref, s_vc.at[b], r_vc.at[b], branch=other)

    def nz(q, side, src, to):
        return copy(src, pan.at[y, q], s_nz.at[q, side], r_nz.at[q], col=to)

    def ny(q, k):
        return copy(pan.at[y, q], pan.at[y, q], s_ny.at[q, k - 1], r_ny.at[q, k - 1], col=along_y(k))

    def ny_recv(q, k):
        ref = pan.at[lax.rem(y + NY - k, NY), q]
        return copy(ref, ref, s_ny.at[q, k - 1], r_ny.at[q, k - 1], col=me)

    lpiv = pltpu.make_async_copy(top.at[:, hrows], piv.at[y, :, hrows], loc.at[0])
    lpan = pltpu.make_async_copy(top, pan.at[y], loc.at[1])

    @pl.when(z == 0)
    def _():
        lpiv.start()
        for b in range(4):
            for k in (4, 5, 3, 6, 2, 7, 1):
                vz(b, k).start()
        lpiv.wait()

    @pl.when(z == br)
    def _():
        lpan.start()
        for q in range(4):
            nz(q, 0, top.at[q], along_z(1)).start()
            nz(q, 1, top.at[q], along_z(7)).start()
        lpan.wait()

    def spread(b):
        @pl.when(z != 0)
        def _():
            ref = piv.at[y, b, hrows]
            copy(ref, ref, s_vz.at[b, 0], r_vz.at[b], col=me).wait_recv()

        for k in (2, 1, 3):
            vy(b, k).start()

    def panel_step(slot):
        q = slot - nhops

        @pl.when(jnp.logical_and(q >= 0, q < 4))
        def _():
            @pl.when(nhops != 0)
            def _():
                nz(q, 0, pan.at[y, q], me).wait_recv()

            @pl.when(nmore)
            def _():
                nz(q, 0, pan.at[y, q], along_z(nstep)).start()

            for k in (2, 1, 3):
                ny(q, k).start()

    def exchange(b):
        for k in (1, 3, 2):
            vy_recv(b, k).wait_recv()
        vc(b).start()

    def rows(b):
        vc_recv(b).wait_recv()
        return jnp.concatenate([piv[j, b] for j in range(b, 4)], axis=1)

    def x_recv(i):
        return copy(rx.at[i], rx.at[i], s_x.at[i], r_x.at[i], branch=br)

    def send2(k):
        to = lax.rem(x + k, 4)
        return copy(sx.at[to], r2.at[k - 1], s_2.at[k - 1], r_2.at[k - 1], branch=2 * to + core)

    def hooks(b):
        def hook(p):
            if p == 7 and b < 3:
                spread(b + 1)
            if p == 12 and b < 3:
                exchange(b + 1)
            if b == 0 and p == 6:
                for i in range(4):
                    x_recv(i).wait_recv()

                @pl.loop(0, 4)
                def _(i):
                    sx[i] = rx[i] + t_ref[pl.ds(4 * (2 * i + core), 4)]

            if b == 0 and p == 9:
                for k in (2, 1, 3):
                    send2(k).start()
            if (b, p) in SLOTS:
                panel_step(SLOTS[b, p])

        return hook

    spread(0)
    exchange(0)
    chol_inverse(rows, s_ref, m_ref, hooks)
    M = m_ref[...]
    F = dot(M, top[...].reshape(PP, HB), ((1,), (0,)))
    fac_ref[...] = F
    Z = dot(M, F, ((0,), (0,)))
    for k in range(1, 4):
        send2(k).wait_recv()
    for q in range(4):
        for k in (1, 3, 2):
            ny_recv(q, k).wait_recv()

    s_ref[:, :HB] = Z

    @pl.loop(0, 4)
    def _(j):
        asm = pf_ref[j] + sx[x, j] + r2[0, j] + r2[1, j] + r2[2, j]
        rowsj = pan[j].reshape(PP, HB)
        out_ref[j] = asm - dot(rowsj, s_ref[:, :HB], ((0,), (0,)))

    for k in range(1, nb):
        rs_send(k).wait_send()
        ag_send(k).wait_send()

    @pl.when(br == 0)
    def _():
        for k in range(1, nb):
            pf_send(k).wait_send()

    for i in range(4):
        x_send(i).wait_send()
    for k in range(1, 4):
        send2(k).wait_send()
        for b in range(4):
            vy(b, k).wait_send()
            ny(b, k).wait_send()

    @pl.when(z == 0)
    def _():
        for b in range(4):
            for k in range(1, NZ):
                vz(b, k).wait_send()

    for b in range(4):
        vc(b).wait_send()

    for q in range(4):
        @pl.when(jnp.logical_or(ndist == 0, nmore))
        def _():
            nz(q, 0, pan.at[y, q], along_z(nstep)).wait_send()

        @pl.when(ndist == 0)
        def _():
            nz(q, 1, pan.at[y, q], along_z(7)).wait_send()

    finish_child()


def fronts(extend_map, front, parent_front):
    dma = pltpu.SemaphoreType.DMA
    return pl.pallas_call(
        front_kernel,
        out_shape=(
            jax.ShapeDtypeStruct((P_SIZE, HB), F32),
            jax.ShapeDtypeStruct((PP, HB), F32),
            jax.ShapeDtypeStruct((4, HB, HB), F32),
        ),
        in_specs=[SMEM, HBM, VMEM],
        out_specs=(VMEM, VMEM, VMEM),
        scratch_shapes=[
            pltpu.VMEM((NH, HB, HB), F32),
            pltpu.VMEM((HB, P_SIZE), F32),
            pltpu.VMEM((NH, HB, HB), F32),
            pltpu.VMEM((NH, HB, P_SIZE), F32),
            pltpu.VMEM((NH, HB, HB), F32),
            pltpu.VMEM((P_SIZE, P_SIZE), F32),
            pltpu.VMEM((P_SIZE, P_SIZE), F32),
            pltpu.VMEM((NH, HB, HB), F32),
            pltpu.VMEM((NH, HB, HB), F32),
            pltpu.SMEM((2, NH), jnp.int32),
            dma((3,)), dma((3,)), dma((7,)), dma((7,)), dma((7,)), dma((7,)),
            dma((8, 2)), dma((8, 2)), dma((8, 2)), dma((8, 2)),
            dma((31,)), dma((31,)), dma((3,)),
            pltpu.VMEM((9, 4, 16, HB), F32),
            pltpu.VMEM((4, 16, HB), F32),
            pltpu.VMEM((4, HB, HB), F32),
            pltpu.VMEM((4, 4, HB, HB), F32),
            pltpu.VMEM((4, 4, HB, HB), F32),
            pltpu.VMEM((4, 4, HB, HB), F32),
            pltpu.VMEM((4, 4, HB, HB), F32),
            pltpu.VMEM((3, 4, HB, HB), F32),
            dma((7,)), dma((7,)), dma((7,)), dma(()), dma((7,)), dma((7,)),
            dma((4,)), dma((4,)), dma((3,)), dma((3,)),
            dma((4, 7)), dma((4,)), dma((4, 3)), dma((4, 3)), dma((4,)), dma((4,)),
            dma((4, 2)), dma((4,)), dma((4, 3)), dma((4, 3)), dma((2,)),
        ],
        compiler_params=pltpu.CompilerParams(
            collective_id=0, has_side_effects=True, vmem_limit_bytes=40 << 20
        ),
        name="fronts",
    )(extend_map, front, parent_front)


def on_device(child_fronts, extend_map, parent_front):
    front = child_fronts[0]
    child_mine, parent_mine, result = fronts(
        extend_map, front.reshape(NH, HB, HB), parent_front.reshape(4, HB, HB)
    )
    return (child_mine[None], parent_mine, result.reshape(parent_front.shape))


def solution(mesh):
    in_specs = (P("branch", None, "col"), P("branch", None), P("branch", "col"))
    out_specs = (P("branch", None, "col"), P(None, "col"), P("branch", "col"))
    return jax.shard_map(
        on_device, mesh=mesh, in_specs=in_specs, out_specs=out_specs, check_vma=False
    )
```

```python
import jax
import jax.numpy as jnp
from jax import lax
from jax.experimental import pallas as pl
from jax.experimental.pallas import tpu as pltpu
from jax.sharding import PartitionSpec as P

BS = 256
P_SIZE = 512
NP = 4096
PP = 512
HB = 128
NZ, NY = 8, 4
NH = NZ * NY
LO = 48
F32 = jnp.float32
HI = lax.Precision.HIGHEST
VMEM = pl.BlockSpec(memory_space=pltpu.VMEM)
SMEM = pl.BlockSpec(memory_space=pltpu.SMEM)
HBM = pl.BlockSpec(memory_space=pltpu.HBM)


def dot(a, b, dims):
    return lax.dot_general(a, b, (dims, ((), ())), precision=HI, preferred_element_type=F32)


def lane(x, i):
    return jnp.broadcast_to(x[:, i : i + 1], (8, 128))


def sub(x, i):
    return jnp.broadcast_to(x[i : i + 1, :], (8, x.shape[1]))


def chol_inv_128(tiles, hook=None):
    row = lax.broadcasted_iota(jnp.int32, (8, 128), 0)
    col = lax.broadcasted_iota(jnp.int32, (8, 128), 1)
    D = list(tiles)
    E = [jnp.where(col == row + 8 * q, 1.0, 0.0).astype(F32) for q in range(16)]
    for p in range(16):
        if hook is not None:
            hook(p)
        a, e = D[p], E[p]
        C = [lane(a, 8 * p + k) for k in range(8)]
        for k in range(8):
            rs = lax.rsqrt(sub(C[k], k))
            l = C[k] * rs
            lm = jnp.where(row > k, l, 0.0)
            for j in range(k + 1, 8):
                C[j] = C[j] - l * sub(l, j)
            ra = sub(a, k) * rs
            re = sub(e, k) * rs
            a = jnp.where(row == k, ra, a - lm * ra)
            e = jnp.where(row == k, re, e - lm * re)
        E[p] = e
        if p < 15:
            at = a.T
            for q in range(p + 1, 16):
                t, u = D[q], E[q]
                for k in range(8):
                    m = jnp.broadcast_to(at[8 * q : 8 * q + 8, k : k + 1], (8, 128))
                    t = t - m * sub(a, k)
                    u = u - m * sub(e, k)
                D[q], E[q] = t, u
    return E


def chol_inverse(rows, s_ref, m_ref, hooks=None):
    m_ref[...] = jnp.zeros((512, 512), F32)
    for b in range(4):
        o = 128 * b
        blk = slice(o, o + 128)
        A = rows(b)
        if b:
            A = A - dot(s_ref[:o, blk], s_ref[:o, o:], ((0,), (0,)))
        tiles = [A[8 * q : 8 * q + 8, :128] for q in range(16)]
        s_ref[blk, o:] = A
        W = jnp.concatenate(chol_inv_128(tiles, None if hooks is None else hooks(b)), axis=0)
        m_ref[blk, blk] = W
        if b < 3:
            s_ref[blk, o + 128 :] = dot(W, s_ref[blk, o + 128 :], ((1,), (0,)))
        if b:
            m_ref[blk, :o] = -dot(W, dot(s_ref[:o, blk], m_ref[:o, :o], ((0,), (0,))), ((1,), (0,)))


def chol_inverse_loop(rows, s_ref, m_ref, hook):
    m_ref[...] = jnp.zeros((512, 512), F32)
    s_ref[...] = jnp.zeros((512, 512), F32)

    @pl.loop(0, 4)
    def _(b):
        hook(b)
        o = pl.multiple_of(128 * b, 128)
        blk = pl.ds(o, 128)
        lead = s_ref[:, blk]
        A = rows(b) - dot(lead, s_ref[...], ((0,), (0,)))
        s_ref[blk, :] = A
        tiles = [s_ref[pl.ds(o + 8 * q, 8), blk] for q in range(16)]
        W = jnp.concatenate(chol_inv_128(tiles), axis=0)
        m_ref[blk, :] = -dot(W, dot(lead, m_ref[...], ((0,), (0,))), ((1,), (0,)))
        m_ref[blk, blk] = W
        s_ref[blk, :] = dot(W, A, ((1,), (0,)))


def child_phase(
    map_ref, front_hbm, g_ref, t_ref,
    front_ref, tt_ref, send_ref, all_ref, recv_ref, s_ref, m_ref, p_ref, tab_ref,
    s0y, r0y, s0z, r0z, s1z, r1z, s1y, r1y, s1f, r1f, sf, rf, loc, first_rows_done,
):
    me = lax.axis_index("col")
    br = lax.axis_index("branch")
    z, y = me // NY, lax.rem(me, NY)
    d = -1

    top = pltpu.make_async_copy(
        front_hbm.at[pl.ds(0, 4)], front_ref.at[pl.ds(0, 4)], loc.at[0]
    )
    top.start()
    rest = pltpu.make_async_copy(
        front_hbm.at[pl.ds(4, NH - 4)], front_ref.at[pl.ds(4, NH - 4)], loc.at[1]
    )
    rest.start()

    def at(zz, yy):
        return lax.rem(zz + 2 * NZ, NZ) * NY + lax.rem(yy + NY, NY)

    barrier = pltpu.get_barrier_semaphore()

    @pl.loop(1, NH)
    def _(k):
        pl.semaphore_signal(barrier, inc=1, device_id={"col": lax.rem(me + k, NH)})

    @pl.loop(1, 8)
    def _(k):
        pl.semaphore_signal(barrier, inc=1, device_id={"branch": lax.rem(br + k, 8)})

    for b in range(NP // BS):
        at_u = jnp.int32(-1)
        for u in range(14):
            at_u = jnp.where(map_ref[0, u] == b, u, at_u)
        keep = (at_u >= 0).astype(jnp.int32)
        src = jnp.where(at_u >= 0, 2 * at_u + 4, 0)
        for part in range(2):
            tab_ref[0, 2 * b + part] = src + part
            tab_ref[1, 2 * b + part] = keep

    top.wait()
    for k in range(4):
        tt_ref[:, 128 * k : 128 * k + 128] = front_ref[k].T

    pl.semaphore_wait(barrier, NH - 1 + 7)

    def copy(src, dst, ss, rs, to):
        return pltpu.make_async_remote_copy(
            src_ref=src, dst_ref=dst, send_sem=ss, recv_sem=rs, device_id={"col": to}
        )

    lo, hi = pl.ds(0, LO), pl.ds(LO, HB - LO)
    mid = (HB - LO) // 2
    half = (pl.ds(LO, mid), pl.ds(LO + mid, mid))
    own = pltpu.make_async_copy(tt_ref, all_ref.at[me], loc.at[2])
    own.start()

    order = [0, 1, -1, 2, -2, 3, -3, 4]
    fwd, bwd = [0, 1, 3, 5, 7], [0, 2, 4, 6]

    def behind(i):
        if isinstance(i, int):
            return order[i]
        return ((i + 1) // 2) * (2 * lax.rem(i, 2) - 1)

    def z1_send(chain, n, src=None):
        i, slot = chain[n], chain[n + 1]
        step = d if chain is fwd else -d
        blk = at(z - order[i] * d, y)
        src = all_ref.at[blk, hi] if src is None else src
        return copy(src, all_ref.at[blk, hi], s1z.at[slot - 1], r1z.at[slot - 1], at(z + step, y))

    def z1_recv(slot):
        ref = all_ref.at[at(z - order[slot] * d, y), hi]
        return copy(ref, ref, s1z.at[slot - 1], r1z.at[slot - 1], me)

    def y1(i, side, src=None):
        blk = at(z - behind(i) * d, y)
        src = all_ref.at[blk, hi] if src is None else src
        return copy(src, all_ref.at[blk, hi], s1y.at[i, side], r1y.at[i, side], at(z, y + 1 - 2 * side))

    def y1_recv(i, side):
        ref = all_ref.at[at(z - behind(i) * d, y - 1 + 2 * side), hi]
        return copy(ref, ref, s1y.at[i, side], r1y.at[i, side], me)

    def y1f(i, side):
        ref = all_ref.at[at(z - behind(i) * d, y - 1 + 2 * side), half[side]]
        return copy(ref, ref, s1f.at[i, side], r1f.at[i, side], at(z, y + 1 - 2 * side))

    def y1f_recv(i, side):
        ref = all_ref.at[at(z - behind(i) * d, y + 2), half[side]]
        return copy(ref, ref, s1f.at[i, side], r1f.at[i, side], me)

    def y0(k, src):
        return copy(src, all_ref.at[me, lo], s0y.at[k - 1], r0y.at[k - 1], at(z, y + k))

    def y0_recv(k):
        ref = all_ref.at[at(z, y - k), lo]
        return copy(ref, ref, s0y.at[k - 1], r0y.at[k - 1], me)

    def bundle(i):
        return all_ref.at[pl.ds(at(z - order[i] * d, 0), NY), lo]

    def z0_send(chain, n):
        i, slot = chain[n], chain[n + 1]
        step = d if chain is fwd else -d
        return copy(bundle(i), bundle(i), s0z.at[slot - 1], r0z.at[slot - 1], at(z + step, y))

    def z0_recv(slot):
        return copy(bundle(slot), bundle(slot), s0z.at[slot - 1], r0z.at[slot - 1], me)

    def fsend(k):
        to = lax.rem(me + k, NH)
        return copy(send_ref.at[to], recv_ref.at[me], sf.at[k - 1], rf.at[k - 1], to)

    def frecv(k):
        frm = lax.rem(me + NH - k, NH)
        return copy(send_ref.at[frm], recv_ref.at[frm], sf.at[k - 1], rf.at[k - 1], frm)

    def picked(h):
        return front_ref[tab_ref[0, h]].T * tab_ref[1, h].astype(F32)

    def prepare(first, last):
        @pl.loop(first, last)
        def _(k):
            h = lax.rem(me + k, NH)
            send_ref[h] = picked(h)

    def start_f(first, last):
        @pl.when(z != 0)
        def _():
            @pl.loop(first, last)
            def _(k):
                fsend(k).start()

    sends = []

    def go(c):
        c.start()
        sends.append(c)

    go(z1_send(fwd, 0, tt_ref.at[hi]))
    go(z1_send(bwd, 0, tt_ref.at[hi]))
    for k in (1, 3, 2):
        go(y0(k, tt_ref.at[lo]))
    for side in (0, 1):
        go(y1(0, side, tt_ref.at[hi]))
    rest.wait()
    prepare(1, 12)
    own.wait()
    for k in (1, 3, 2):
        y0_recv(k).wait_recv()
    go(z0_send(fwd, 0))
    go(z0_send(bwd, 0))
    for n in range(1, 5):
        for chain in (fwd, bwd):
            if n < len(chain):
                slot = chain[n]
                z1_recv(slot).wait_recv()
                if n + 1 < len(chain):
                    go(z1_send(chain, n))
                for side in (0, 1):
                    go(y1(slot, side))
        if n == 1:
            prepare(12, NH)
            recv_ref[me] = picked(me)
        for chain in (fwd, bwd):
            if n < len(chain):
                z0_recv(chain[n]).wait_recv()
                if n + 1 < len(chain):
                    go(z0_send(chain, n))
        start_f(1 + 4 * (n - 1), 1 + 4 * n)

    dist = lax.rem(z * d + NZ, NZ)
    i0 = jnp.where(dist <= 4, jnp.where(dist == 0, 0, 2 * dist - 1), 2 * (NZ - dist))
    for side in (0, 1):
        y1_recv(i0, side).wait_recv()
        y1f(i0, side).start()
    start_f(17, NH)
    for side in (0, 1):
        y1f_recv(i0, side).wait_recv()

    def forward(b):
        for n in range(2):
            i = 2 * b + n

            @pl.when(i != i0)
            def _():
                for side in (0, 1):
                    y1_recv(i, side).wait_recv()
                    y1f(i, side).start()

    chol_inverse_loop(lambda b: all_ref[b], s_ref, m_ref, forward)
    M = m_ref[...]
    g_ref[...] = dot(M, all_ref[me], ((1,), (1,)))

    @pl.loop(0, 8)
    def _(i):
        @pl.when(i != i0)
        def _():
            for side in (0, 1):
                y1f_recv(i, side).wait_recv()

    Y = dot(M, all_ref[tab_ref[0, me]], ((1,), (1,)))
    s_ref[:, :HB] = dot(M, Y, ((0,), (0,)))

    @pl.loop(0, NH // 4)
    def _(i):
        rows = all_ref[pl.ds(4 * i, 4)].reshape(4 * HB, P_SIZE)
        p_ref[pl.ds(4 * i, 4)] = dot(rows, s_ref[:, :HB], ((1,), (0,))).reshape(4, HB, HB)

    @pl.loop(1, NH)
    def _(k):
        @pl.when(lax.rem(me + NH - k, NH) >= NY)
        def _():
            frecv(k).wait_recv()

    keep_me = tab_ref[1, me].astype(F32)

    def strip(first, last):
        @pl.loop(first, last)
        def _(p):
            q = tab_ref[0, p]
            keep = tab_ref[1, p].astype(F32)
            t_ref[p] = keep * (recv_ref[q] - keep_me * p_ref[q])

    strip(0, 4)
    first_rows_done()
    strip(4, NH)

    def finish():
        for c in sends:
            c.wait_send()

        @pl.loop(0, 8)
        def _(i):
            for side in (0, 1):
                y1f(i, side).wait_send()

        @pl.when(z != 0)
        def _():
            @pl.loop(1, NH)
            def _(k):
                fsend(k).wait_send()

    return finish


SLOTS = {(0, 2): 0, (0, 9): 1, (1, 0): 2, (1, 7): 3, (1, 14): 4, (2, 5): 5, (2, 12): 6, (3, 3): 7}


def front_kernel(
    map_ref, front_hbm, pf_ref, g_ref, fac_ref, out_ref,
    front_ref, tt_ref, send_ref, all_ref, recv_ref, s_ref, m_ref, p_ref, t_ref, tab_ref,
    s0y, r0y, s0z, r0z, s1z, r1z, s1y, r1y, s1f, r1f, sf, rf, cloc,
    rtop, part, top, piv, pan, rx, sx, r2,
    s_rs, r_rs, s_pf, r_pf, s_ag, r_ag, s_x, r_x, s_2, r_2,
    s_vz, r_vz, s_vy, r_vy, s_vc, r_vc, s_nz, r_nz, s_ny, r_ny, loc,
):
    br, me = lax.axis_index("branch"), lax.axis_index("col")
    x, core = br // 2, lax.rem(br, 2)
    z, y = me // NY, lax.rem(me, NY)
    nb = 8

    def along_z(k):
        return lax.rem(z + k, NZ) * NY + y

    def along_y(k):
        return z * NY + lax.rem(y + k, NY)

    def copy(src, dst, ss, rs, **to):
        return pltpu.make_async_remote_copy(
            src_ref=src, dst_ref=dst, send_sem=ss, recv_sem=rs, device_id=to
        )

    def piece(b):
        return pl.ds(pl.multiple_of(16 * b, 16), 16)

    def rs_send(k):
        to = lax.rem(br + k, nb)
        return copy(t_ref.at[pl.ds(0, 4), piece(to)], rtop.at[br], s_rs.at[k - 1], r_rs.at[k - 1], branch=to)

    def rs_recv(k):
        frm = lax.rem(br + nb - k, nb)
        return copy(rtop.at[frm], rtop.at[frm], s_rs.at[k - 1], r_rs.at[k - 1], branch=frm)

    def pf_send(k):
        return copy(pf_ref.at[:, piece(k)], rtop.at[nb], s_pf.at[k - 1], r_pf, branch=jnp.int32(k))

    def start_rows():
        for k in range(1, nb):
            rs_send(k).start()

    finish_child = child_phase(
        map_ref, front_hbm, g_ref, t_ref,
        front_ref, tt_ref, send_ref, all_ref, recv_ref, s_ref, m_ref, p_ref, tab_ref,
        s0y, r0y, s0z, r0z, s1z, r1z, s1y, r1y, s1f, r1f, sf, rf, cloc, start_rows,
    )

    @pl.when(br == 0)
    def _():
        for k in range(1, nb):
            pf_send(k).start()

    def x_send(i):
        grp = 2 * i + 1 - core
        return copy(t_ref.at[pl.ds(4 * grp, 4)], rx.at[i], s_x.at[i], r_x.at[i], branch=br + 1 - 2 * core)

    for i in range(4):
        x_send(i).start()

    own = t_ref[0:4, piece(br), :]
    for k in range(1, nb):
        rs_recv(k).wait_recv()
        own = own + rtop[lax.rem(br + nb - k, nb)]
    part[...] = own

    @pl.when(br == 0)
    def _():
        part[...] += pf_ref[:, 0:16, :]

    @pl.when(br != 0)
    def _():
        copy(rtop.at[nb], rtop.at[nb], s_pf.at[0], r_pf, branch=jnp.int32(0)).wait_recv()
        part[...] += rtop[nb]

    def ag_send(k):
        to = lax.rem(br + k, nb)
        return copy(part, top.at[:, piece(br)], s_ag.at[k - 1], r_ag.at[k - 1], branch=to)

    def ag_recv(k):
        ref = top.at[:, piece(lax.rem(br + nb - k, nb))]
        return copy(part, ref, s_ag.at[k - 1], r_ag.at[k - 1], branch=br)

    for k in range(1, nb):
        ag_send(k).start()
    top[:, piece(br), :] = part[...]
    for k in range(1, nb):
        ag_recv(k).wait_recv()

    def chain(dist):
        step = jnp.where(dist <= 4, 1, NZ - 1)
        return step, jnp.logical_and(dist != 0, jnp.logical_and(dist != 4, dist != 5))

    ndist = lax.rem(z + NZ - br, NZ)
    nstep, nmore = chain(ndist)
    nhops = jnp.minimum(ndist, NZ - ndist)
    hrows = pl.ds(pl.multiple_of(64 * core, 64), 64)
    orows = pl.ds(pl.multiple_of(64 - 64 * core, 64), 64)
    other = br + 1 - 2 * core

    def vz(b, k):
        return copy(top.at[b, hrows], piv.at[y, b, hrows], s_vz.at[b, k - 1], r_vz.at[b], col=along_z(k))

    def vy(b, k):
        ref = piv.at[y, b, hrows]
        return copy(ref, ref, s_vy.at[b, k - 1], r_vy.at[b, k - 1], col=along_y(k))

    def vy_recv(b, k):
        ref = piv.at[lax.rem(y + NY - k, NY), b, hrows]
        return copy(ref, ref, s_vy.at[b, k - 1], r_vy.at[b, k - 1], col=me)

    def vc(b):
        ref = piv.at[:, b, hrows]
        return copy(ref, ref, s_vc.at[b], r_vc.at[b], branch=other)

    def vc_recv(b):
        ref = piv.at[:, b, orows]
        return copy(ref, ref, s_vc.at[b], r_vc.at[b], branch=other)

    def nz(q, side, src, to):
        return copy(src, pan.at[y, q], s_nz.at[q, side], r_nz.at[q], col=to)

    def ny(q, k):
        return copy(pan.at[y, q], pan.at[y, q], s_ny.at[q, k - 1], r_ny.at[q, k - 1], col=along_y(k))

    def ny_recv(q, k):
        ref = pan.at[lax.rem(y + NY - k, NY), q]
        return copy(ref, ref, s_ny.at[q, k - 1], r_ny.at[q, k - 1], col=me)

    lpiv = pltpu.make_async_copy(top.at[:, hrows], piv.at[y, :, hrows], loc.at[0])
    lpan = pltpu.make_async_copy(top, pan.at[y], loc.at[1])

    @pl.when(z == 0)
    def _():
        lpiv.start()
        for b in range(4):
            for k in (4, 5, 3, 6, 2, 7, 1):
                vz(b, k).start()
        lpiv.wait()

    @pl.when(z == br)
    def _():
        lpan.start()
        for q in range(4):
            nz(q, 0, top.at[q], along_z(1)).start()
            nz(q, 1, top.at[q], along_z(7)).start()
        lpan.wait()

    def spread(b):
        @pl.when(z != 0)
        def _():
            ref = piv.at[y, b, hrows]
            copy(ref, ref, s_vz.at[b, 0], r_vz.at[b], col=me).wait_recv()

        for k in (2, 1, 3):
            vy(b, k).start()

    def panel_step(slot):
        q = slot - nhops

        @pl.when(jnp.logical_and(q >= 0, q < 4))
        def _():
            @pl.when(nhops != 0)
            def _():
                nz(q, 0, pan.at[y, q], me).wait_recv()

            @pl.when(nmore)
            def _():
                nz(q, 0, pan.at[y, q], along_z(nstep)).start()

            for k in (2, 1, 3):
                ny(q, k).start()

    def exchange(b):
        for k in (1, 3, 2):
            vy_recv(b, k).wait_recv()
        vc(b).start()

    def rows(b):
        vc_recv(b).wait_recv()
        return jnp.concatenate([piv[j, b] for j in range(b, 4)], axis=1)

    def x_recv(i):
        return copy(rx.at[i], rx.at[i], s_x.at[i], r_x.at[i], branch=br)

    def send2(k):
        to = lax.rem(x + k, 4)
        return copy(sx.at[to], r2.at[k - 1], s_2.at[k - 1], r_2.at[k - 1], branch=2 * to + core)

    def hooks(b):
        def hook(p):
            if p == 7 and b < 3:
                spread(b + 1)
            if p == 12 and b < 3:
                exchange(b + 1)
            if b == 0 and p == 6:
                for i in range(4):
                    x_recv(i).wait_recv()

                @pl.loop(0, 4)
                def _(i):
                    sx[i] = rx[i] + t_ref[pl.ds(4 * (2 * i + core), 4)]

            if b == 0 and p == 9:
                for k in (2, 1, 3):
                    send2(k).start()
            if (b, p) in SLOTS:
                panel_step(SLOTS[b, p])

        return hook

    spread(0)
    exchange(0)
    chol_inverse(rows, s_ref, m_ref, hooks)
    M = m_ref[...]
    F = dot(M, top[...].reshape(PP, HB), ((1,), (0,)))
    fac_ref[...] = F
    Z = dot(M, F, ((0,), (0,)))
    for k in range(1, 4):
        send2(k).wait_recv()
    for q in range(4):
        for k in (1, 3, 2):
            ny_recv(q, k).wait_recv()

    s_ref[:, :HB] = Z

    @pl.loop(0, 4)
    def _(j):
        asm = pf_ref[j] + sx[x, j] + r2[0, j] + r2[1, j] + r2[2, j]
        rowsj = pan[j].reshape(PP, HB)
        out_ref[j] = asm - dot(rowsj, s_ref[:, :HB], ((0,), (0,)))

    for k in range(1, nb):
        rs_send(k).wait_send()
        ag_send(k).wait_send()

    @pl.when(br == 0)
    def _():
        for k in range(1, nb):
            pf_send(k).wait_send()

    for i in range(4):
        x_send(i).wait_send()
    for k in range(1, 4):
        send2(k).wait_send()
        for b in range(4):
            vy(b, k).wait_send()
            ny(b, k).wait_send()

    @pl.when(z == 0)
    def _():
        for b in range(4):
            for k in range(1, NZ):
                vz(b, k).wait_send()

    for b in range(4):
        vc(b).wait_send()

    for q in range(4):
        @pl.when(jnp.logical_or(ndist == 0, nmore))
        def _():
            nz(q, 0, pan.at[y, q], along_z(nstep)).wait_send()

        @pl.when(ndist == 0)
        def _():
            nz(q, 1, pan.at[y, q], along_z(7)).wait_send()

    finish_child()


def fronts(extend_map, front, parent_front):
    dma = pltpu.SemaphoreType.DMA
    return pl.pallas_call(
        front_kernel,
        out_shape=(
            jax.ShapeDtypeStruct((P_SIZE, HB), F32),
            jax.ShapeDtypeStruct((PP, HB), F32),
            jax.ShapeDtypeStruct((4, HB, HB), F32),
        ),
        in_specs=[SMEM, HBM, VMEM],
        out_specs=(VMEM, VMEM, VMEM),
        scratch_shapes=[
            pltpu.VMEM((NH, HB, HB), F32),
            pltpu.VMEM((HB, P_SIZE), F32),
            pltpu.VMEM((NH, HB, HB), F32),
            pltpu.VMEM((NH, HB, P_SIZE), F32),
            pltpu.VMEM((NH, HB, HB), F32),
            pltpu.VMEM((P_SIZE, P_SIZE), F32),
            pltpu.VMEM((P_SIZE, P_SIZE), F32),
            pltpu.VMEM((NH, HB, HB), F32),
            pltpu.VMEM((NH, HB, HB), F32),
            pltpu.SMEM((2, NH), jnp.int32),
            dma((3,)), dma((3,)), dma((7,)), dma((7,)), dma((7,)), dma((7,)),
            dma((8, 2)), dma((8, 2)), dma((8, 2)), dma((8, 2)),
            dma((31,)), dma((31,)), dma((3,)),
            pltpu.VMEM((9, 4, 16, HB), F32),
            pltpu.VMEM((4, 16, HB), F32),
            pltpu.VMEM((4, HB, HB), F32),
            pltpu.VMEM((4, 4, HB, HB), F32),
            pltpu.VMEM((4, 4, HB, HB), F32),
            pltpu.VMEM((4, 4, HB, HB), F32),
            pltpu.VMEM((4, 4, HB, HB), F32),
            pltpu.VMEM((3, 4, HB, HB), F32),
            dma((7,)), dma((7,)), dma((7,)), dma(()), dma((7,)), dma((7,)),
            dma((4,)), dma((4,)), dma((3,)), dma((3,)),
            dma((4, 7)), dma((4,)), dma((4, 3)), dma((4, 3)), dma((4,)), dma((4,)),
            dma((4, 2)), dma((4,)), dma((4, 3)), dma((4, 3)), dma((2,)),
        ],
        compiler_params=pltpu.CompilerParams(
            collective_id=0, has_side_effects=True, vmem_limit_bytes=40 << 20
        ),
        name="fronts",
    )(extend_map, front, parent_front)


def on_device(child_fronts, extend_map, parent_front):
    front = child_fronts[0]
    child_mine, parent_mine, result = fronts(
        extend_map, front.reshape(NH, HB, HB), parent_front.reshape(4, HB, HB)
    )
    return (child_mine[None], parent_mine, result.reshape(parent_front.shape))


def solution(mesh):
    in_specs = (P("branch", None, "col"), P("branch", None), P("branch", "col"))
    out_specs = (P("branch", None, "col"), P(None, "col"), P("branch", "col"))
    return jax.shard_map(
        on_device, mesh=mesh, in_specs=in_specs, out_specs=out_specs, check_vma=False
    )
```
